128 devices in a mesh: row: 8 (over x, core), col: 16 (over y, z).
Axes of the slice: x: 4, y: 4, z: 4, core: 2. Of those that a mesh axis runs over, the one named last changes fastest.
Arguments:
- amp_ladder: bfloat16 [8, 32, 128, 32, 128], P('row', 'col'), may hold values from -6 to 6
- integrals: bfloat16 [8, 24, 128, 32, 128], P(None, 'row', None, 'col'), may hold values from -0.09375 to 0.09375
- residual_in: float32 [8, 24, 128, 32, 128], P(None, 'row', None, 'col'), may hold values from -6 to 6
Outputs:
- residual_out: float32 [8, 24, 128, 32, 128], P(None, 'row', None, 'col')
The draws below stay inside these ranges and needn't reach their ends.
All inputs are finite; a program needn't handle non-finite values.
Results may differ from the reference program's by a relative error of at most 0.0003.
Values may be sent and summed in bfloat16 or wider, within the bound.
A program may use at most 192 MiB of HBM per device.

```python
import jax
import jax.numpy as jnp
from jax import lax

IRREPS = 8
BLK = 128
RPI = 24
KPI = 32
CPI = 32


def shard_levels(key, dims, split, low, high):
    def one(position, parts):
        steps = jax.random.uniform(jax.random.fold_in(jax.random.fold_in(key, 6), position), (parts,), jnp.float32, low / len(split), high / len(split))
        return jnp.repeat(jnp.exp(steps), dims[position] // parts).reshape((-1,) + (1,) * (len(dims) - position - 1))

    level = one(*split[0])
    for cut in split[1:]:
        level = level * one(*cut)
    return level


def scatter_about(own_key, extent, scale, bound, split=(), held_as=jnp.bfloat16):
    level = shard_levels(own_key, extent, split, -0.22, 0.18) if split else 1.0
    result = jax.random.normal(own_key, extent, jnp.float32) * scale * level
    return jnp.minimum(jnp.maximum(result, -bound), bound).astype(held_as)


def setup_inputs(seed: int = 0) -> dict:
    key_of = jax.random.split(jax.random.key(seed), 4)
    amp_ladder = scatter_about(key_of[0], (IRREPS, KPI, BLK, CPI, BLK), 1.0, 6.0, ((0, 8), (1, 16)))
    integrals = scatter_about(key_of[1], (IRREPS, RPI, BLK, KPI, BLK), (KPI * BLK) ** -0.5, 0.09375, ((1, 8), (3, 16)))
    residual_in = scatter_about(key_of[2], (IRREPS, RPI, BLK, CPI, BLK), 1.0, 6.0, ((1, 8), (3, 16)), jnp.float32)
    return dict(amp_ladder=amp_ladder, integrals=integrals, residual_in=residual_in)


def irrep_cycle(pair):
    left, right = pair
    rows = left.shape[0] * left.shape[1]
    inner = left.shape[2] * left.shape[3]
    cols = right.shape[2] * right.shape[3]
    product = jnp.dot(left.astype(jnp.float32).reshape(rows, inner), right.astype(jnp.float32).reshape(inner, cols), precision=lax.Precision.HIGHEST, preferred_element_type=jnp.float32)
    return product.reshape(left.shape[0], left.shape[1], right.shape[2], right.shape[3])


def reference(amp_ladder, integrals, residual_in):
    cycle = lax.map(irrep_cycle, (integrals, amp_ladder))
    return residual_in + cycle
```

```python
import functools

import jax
import jax.numpy as jnp
from jax import lax
from jax.experimental import pallas as pl
from jax.experimental.pallas import tpu as pltpu
from jax.sharding import PartitionSpec as P

MESH = pl.DeviceIdType.MESH
JXOR = (1, 2, 0, 3)


def kernel(a_in, b_in, res, out, abuf, bbuf, cp, cr, cf, obuf,
           a_s, a_r, g_s, g_r, b_s, b_r, f_s, p_s, p_r, o_s, o_r):
    row, col = lax.axis_index("row"), lax.axis_index("col")
    x, c, y, z = row // 2, row % 2, col // 4, col % 4
    par = z // 2
    mir = 3 - z
    buddy = z + 1 - 2 * (z % 2)

    def dev(xx, cc, yy, zz):
        return (xx * 2 + cc, yy * 4 + zz)

    def xor(zz, j):
        lo, hi = zz % 2, zz // 2
        m = JXOR[j]
        lo = 1 - lo if m % 2 else lo
        hi = 1 - hi if m // 2 else hi
        return hi * 2 + lo

    def remote(src, dst, ss, rs, d):
        return pltpu.make_async_remote_copy(src, dst, ss, rs, device_id=d, device_id_type=MESH)

    barrier = pltpu.get_barrier_semaphore()
    peers = []
    for d in range(4):
        for zz in (z, mir):
            if d or zz is mir:
                peers.append(dev((x + d) % 4, c, y, zz))
            if d:
                peers.append(dev(x, c, (y + d) % 4, zz))
    peers.append(dev(x, 1 - c, y, z))
    peers.append(dev(x, c, y, buddy))
    for d in peers:
        pl.semaphore_signal(barrier, inc=1, device_id=d, device_id_type=MESH)
    pl.semaphore_wait(barrier, len(peers))

    sends = []

    def b_start(j):
        for dy in (1, 3, 2, 0):
            yd = (y + dy) % 4

            def go(zd, zz, local):
                src = b_in.at[yd * 4 + xor(zd, j)]
                dst = bbuf.at[j, pl.ds(pl.multiple_of((y * 2 + zz) * 256, 256), 256)]
                if local:
                    pltpu.make_async_copy(src, dst, b_r.at[y, zz, j]).start()
                else:
                    remote(src, dst, b_s.at[dy, j], b_r.at[y, zz, j], dev(x, c, yd, zd)).start()

            @pl.when(c == par)
            def _():
                go(z, 0, dy == 0)

            @pl.when(c != par)
            def _():
                go(mir, 1, False)

    def b_wait_sends():
        for j in range(4):
            for dy in range(4):
                cp_ = remote(b_in.at[0], bbuf.at[0, pl.ds(0, 256)], b_s.at[dy, j], b_r.at[0, 0, j], dev(x, c, y, z))
                if dy == 0:
                    @pl.when(c != par)
                    def _():
                        cp_.wait_send()
                else:
                    cp_.wait_send()

    def b_arrive(j):
        for dy in (0, 1, 3, 2):
            ys = (y + dy) % 4
            for zz in range(2):
                blk = bbuf.at[j, pl.ds(pl.multiple_of((ys * 2 + zz) * 256, 256), 256)]
                fw = remote(blk, blk, f_s.at[dy, zz, j], b_r.at[ys, zz, j], dev(x, 1 - c, y, z))
                fw.wait_recv()

                @pl.when(c == par)
                def _():
                    fw.start()

    def b_forward_wait():
        @pl.when(c == par)
        def _():
            for j in range(4):
                for dy in range(4):
                    for zz in range(2):
                        blk = bbuf.at[j, pl.ds(0, 256)]
                        remote(blk, blk, f_s.at[dy, zz, j], b_r.at[0, zz, j], dev(x, 1 - c, y, z)).wait_send()

    def a_copy(dx, zz):
        hx = (x + 4 - dx) % 4
        zd = mir if zz else z
        src = a_in.at[hx * 2 + zd // 2]
        dst = abuf.at[x, y * 2 + zz]
        if dx == 0 and zz == 0:
            return pltpu.make_async_copy(src, dst, a_r.at[x, 0])
        return remote(src, dst, a_s.at[dx, zz], a_r.at[x, zz], dev(hx, c, y, zd))

    def a_start(dx):
        for zz in (1, 0):
            cp_ = a_copy(dx, zz)
            cp_.start()
            if dx or zz:
                sends.append(cp_)

    def a_arrive(s):
        xs = (x + s) % 4
        for zz in range(2):
            blk = abuf.at[xs, y * 2 + zz]
            if s == 0 and zz == 0:
                a_copy(0, 0).wait()
            else:
                remote(blk, blk, a_s.at[s, zz], a_r.at[xs, zz], dev(x, c, y, mir)).wait_recv()

    def gather_copy(s, up, ys, zz, frm, k):
        xs = (x + s) % 4
        blk = abuf.at[xs, ys * 2 + zz]
        to = (y + 1) % 4 if up else (y + 3) % 4
        return remote(blk, blk, g_s.at[s, k], g_r.at[s, frm, zz], dev(x, c, to, z))

    def gather_start(s):
        for k, (up, zz) in enumerate(((True, 0), (False, 1), (True, 1), (False, 0))):
            cp_ = gather_copy(s, up, y, zz, 0 if up else 1, k)
            cp_.start()
            sends.append(cp_)

    def gather_wait(s, frm, zz):
        ys = (y + (3, 1, 2)[frm]) % 4
        blk = abuf.at[(x + s) % 4, ys * 2 + zz]
        remote(blk, blk, g_s.at[s, 0], g_r.at[s, frm, zz], dev(x, c, y, mir)).wait_recv()

    def gather_forward(s):
        gather_wait(s, 0, 0)
        f1 = gather_copy(s, True, (y + 3) % 4, 0, 2, 4)
        f1.start()
        gather_wait(s, 1, 1)
        f2 = gather_copy(s, False, (y + 1) % 4, 1, 2, 5)
        f2.start()
        sends.extend((f1, f2))

    def gather_rest(s):
        gather_wait(s, 0, 1)
        gather_wait(s, 1, 0)
        gather_wait(s, 2, 0)
        gather_wait(s, 2, 1)

    def product(s, j, t):
        xs = (x + s) % 4
        rows = pl.ds(pl.multiple_of(t * 128, 128), 128)
        left = jnp.concatenate([abuf[xs, k, rows, :] for k in range(8)], axis=1)
        return jnp.dot(left, bbuf[j], preferred_element_type=jnp.float32)

    def partial_send(s):
        for j in range(2):
            @pl.loop(0, 3)
            def _(t):
                cp[s, j, pl.ds(pl.multiple_of(t * 128, 128), 128), :] = product(s, j, t)
            cp_ = remote(cp.at[s, j], cr.at[s, j], p_s.at[s, j], p_r.at[s, j], dev(x, c, y, buddy))
            cp_.start()
            sends.append(cp_)

    def finish(s):
        xd = (x + s) % 4
        h = x * 2 + par
        for j in (1, 0):
            remote(cp.at[s, j], cr.at[s, j], p_s.at[s, j], p_r.at[s, j], dev(x, c, y, buddy)).wait_recv()
            local = s == 0 and j == 0

            @pl.loop(0, 3)
            def _(t):
                rows = pl.ds(pl.multiple_of(t * 128, 128), 128)
                total = product(s, j + 2, t) + cr[s, j, rows, :]
                for q in range(2):
                    part = total[:, q * 128:(q + 1) * 128]
                    lines = pl.ds(t * 256 + q, 128, stride=2)
                    if local:
                        obuf[h, lines, :] = part
                    else:
                        cf[s, j, lines, :] = part
            if not local:
                zd = mir if j else z
                cp_ = remote(cf.at[s, j], obuf.at[h], o_s.at[s, j], o_r.at[h], dev(xd, c, y, zd))
                cp_.start()
                sends.append(cp_)

    a_start(0)
    b_start(0)
    b_start(1)
    a_start(1)
    b_start(2)
    b_start(3)
    a_start(2)
    a_start(3)
    a_arrive(0)
    gather_start(0)
    b_arrive(0)
    b_arrive(1)
    gather_forward(0)
    a_arrive(1)
    gather_start(1)
    b_arrive(2)
    b_arrive(3)
    for s in range(4):
        gather_rest(s)
        if s + 1 < 4:
            gather_forward(s + 1)
        if s + 2 < 4:
            a_arrive(s + 2)
            gather_start(s + 2)
        partial_send(s)
        if s:
            finish(s - 1)
    finish(3)

    for dx in range(4):
        for zz in range(2):
            xs = (x + dx) % 4
            h = xs * 2 + (par if zz == 0 else 1 - par)
            if dx or zz:
                remote(cf.at[0, 0], obuf.at[h], o_s.at[0, 0], o_r.at[h], dev(x, c, y, mir)).wait_recv()
            out[h] = res[h] + obuf[h]
    for cp_ in sends:
        cp_.wait_send()
    b_wait_sends()
    b_forward_wait()


def per_device(amp, integrals, residual_in):
    irreps, blocks, blk, kb, _ = integrals.shape
    rows = blocks * blk
    left = integrals.reshape(irreps, rows, kb * blk)
    right = amp.reshape(kb * blk, 16, 2 * blk).transpose(1, 0, 2)
    res = residual_in.reshape(irreps, rows * 2, blk)
    dma = pltpu.SemaphoreType.DMA
    out = pl.pallas_call(
        kernel,
        out_shape=jax.ShapeDtypeStruct(res.shape, jnp.float32),
        in_specs=[pl.BlockSpec(memory_space=pl.ANY), pl.BlockSpec(memory_space=pl.ANY), pl.BlockSpec(memory_space=pltpu.VMEM)],
        out_specs=pl.BlockSpec(memory_space=pltpu.VMEM),
        scratch_shapes=[
            pltpu.VMEM((4, 8, rows, 256), jnp.bfloat16),
            pltpu.VMEM((4, 2048, 256), jnp.bfloat16),
            pltpu.VMEM((4, 2, rows, 256), jnp.float32),
            pltpu.VMEM((4, 2, rows, 256), jnp.float32),
            pltpu.VMEM((4, 2, rows * 2, blk), jnp.float32),
            pltpu.VMEM((8, rows * 2, blk), jnp.float32),
            dma((4, 2)), dma((4, 2)),
            dma((4, 6)), dma((4, 3, 2)),
            dma((4, 4)), dma((4, 2, 4)), dma((4, 2, 4)),
            dma((4, 2)), dma((4, 2)),
            dma((4, 2)), dma((8,)),
        ],
        compiler_params=pltpu.CompilerParams(collective_id=0, has_side_effects=True, vmem_limit_bytes=60 << 20),
    )(left, right, res)
    return out.reshape(residual_in.shape)


def solution(mesh):
    placed = (
        P("row", "col", None, None, None),
        P(None, "row", None, "col", None),
        P(None, "row", None, "col", None),
    )
    return jax.shard_map(
        per_device,
        mesh=mesh,
        in_specs=placed,
        out_specs=P(None, "row", None, "col", None),
        check_vma=False,
    )
```

```python
import jax
import jax.numpy as jnp
from jax import lax
from jax.experimental import pallas as pl
from jax.experimental.pallas import tpu as pltpu
from jax.sharding import PartitionSpec as P

MESH = pl.DeviceIdType.MESH
MODE = "full"
JXOR = (1, 2, 0, 3)
CHUNKS = ((0, 0), (1, 0), (1, 1), (2, 0), (2, 1), (3, 0), (3, 1), (0, 1))
NQ = len(CHUNKS)
LAG = 2
AHEAD = 2


def kernel(a_in, b_in, out, abuf, bbuf, cp, cr, cf,
           a_s, a_r, g_s, g_r, b_s, b_r, f_s, p_s, p_r, o_s, o_r):
    row, col = lax.axis_index("row"), lax.axis_index("col")
    x, c, y, z = row // 2, row % 2, col // 4, col % 4
    par = z // 2
    mir = 3 - z
    buddy = z + 1 - 2 * (z % 2)
    half = abuf.shape[2] // 2

    def dev(xx, cc, yy, zz):
        return (xx * 2 + cc, yy * 4 + zz)

    def xor(zz, j):
        lo, hi = zz % 2, zz // 2
        m = JXOR[j]
        lo = 1 - lo if m % 2 else lo
        hi = 1 - hi if m // 2 else hi
        return hi * 2 + lo

    def remote(src, dst, ss, rs, d):
        return pltpu.make_async_remote_copy(src, dst, ss, rs, device_id=d, device_id_type=MESH)

    barrier = pltpu.get_barrier_semaphore()
    peers = []
    for d in range(4):
        for zz in (z, mir):
            if d or zz is mir:
                peers.append(dev((x + d) % 4, c, y, zz))
            if d:
                peers.append(dev(x, c, (y + d) % 4, zz))
    peers.append(dev(x, 1 - c, y, z))
    peers.append(dev(x, c, y, buddy))
    for d in peers:
        pl.semaphore_signal(barrier, inc=1, device_id=d, device_id_type=MESH)
    pl.semaphore_wait(barrier, len(peers))

    sends = []

    def b_block(j, ys, zz):
        return bbuf.at[j, pl.ds(pl.multiple_of((ys * 2 + zz) * 256, 256), 256)]

    def b_start(j):
        for dy in (1, 3, 2, 0):
            yd = (y + dy) % 4

            def go(zd, zz, local):
                src = b_in.at[yd * 4 + xor(zd, j)]
                dst = b_block(j, y, zz)
                if local:
                    pltpu.make_async_copy(src, dst, b_r.at[y, zz, j]).start()
                else:
                    remote(src, dst, b_s.at[dy, j], b_r.at[y, zz, j], dev(x, c, yd, zd)).start()

            @pl.when(c == par)
            def _():
                go(z, 0, dy == 0)

            @pl.when(c != par)
            def _():
                go(mir, 1, False)

    def b_wait_sends():
        for j in range(4):
            for dy in range(4):
                cp_ = remote(b_in.at[0], b_block(0, 0, 0), b_s.at[dy, j], b_r.at[0, 0, j], dev(x, c, y, mir))
                if dy == 0:
                    @pl.when(c != par)
                    def _():
                        cp_.wait_send()
                else:
                    cp_.wait_send()

    def b_arrive(j):
        for dy in (0, 1, 3, 2):
            ys = (y + dy) % 4
            for zz in range(2):
                blk = b_block(j, ys, zz)
                fw = remote(blk, blk, f_s.at[dy, zz, j], b_r.at[ys, zz, j], dev(x, 1 - c, y, z))
                fw.wait_recv()

                @pl.when(c == par)
                def _():
                    fw.start()

    def b_forward_wait():
        @pl.when(c == par)
        def _():
            for j in range(4):
                for dy in range(4):
                    for zz in range(2):
                        blk = b_block(j, 0, 0)
                        remote(blk, blk, f_s.at[dy, zz, j], b_r.at[0, zz, j], dev(x, 1 - c, y, z)).wait_send()

    def a_copy(dx, r, zz):
        hx = (x + 4 - dx) % 4
        zd = mir if zz else z
        rows = pl.ds(r * half, half)
        src = a_in.at[hx * 2 + zd // 2, rows]
        dst = abuf.at[x, y * 2 + zz, rows]
        if dx == 0 and zz == 0:
            return pltpu.make_async_copy(src, dst, a_r.at[x, 0, r])
        return remote(src, dst, a_s.at[dx, zz, r], a_r.at[x, zz, r], dev(hx, c, y, zd))

    def a_start(q):
        dx, r = CHUNKS[q]
        for zz in (1, 0):
            cp_ = a_copy(dx, r, zz)
            cp_.start()
            if dx or zz:
                sends.append(cp_)

    def a_block(s, r, ys, zz):
        return abuf.at[(x + s) % 4, ys * 2 + zz, pl.ds(r * half, half)]

    def a_arrive(q):
        s, r = CHUNKS[q]
        for zz in range(2):
            if s == 0 and zz == 0:
                a_copy(0, r, 0).wait()
            else:
                blk = a_block(s, r, y, zz)
                remote(blk, blk, a_s.at[s, zz, r], a_r.at[(x + s) % 4, zz, r], dev(x, c, y, mir)).wait_recv()

    def gather_copy(q, up, ys, zz, frm, k):
        blk = a_block(*CHUNKS[q], ys, zz)
        to = (y + 1) % 4 if up else (y + 3) % 4
        return remote(blk, blk, g_s.at[q, k], g_r.at[q, frm, zz], dev(x, c, to, z))

    def gather_start(q):
        a_arrive(q)
        for k, (up, zz) in enumerate(((True, 0), (False, 1), (True, 1), (False, 0))):
            cp_ = gather_copy(q, up, y, zz, 0 if up else 1, k)
            cp_.start()
            sends.append(cp_)

    def gather_wait(q, frm, zz):
        blk = a_block(*CHUNKS[q], (y + (3, 1, 2)[frm]) % 4, zz)
        remote(blk, blk, g_s.at[q, 0], g_r.at[q, frm, zz], dev(x, c, y, mir)).wait_recv()

    def gather_forward(q):
        gather_wait(q, 0, 0)
        f1 = gather_copy(q, True, (y + 3) % 4, 0, 2, 4)
        f1.start()
        gather_wait(q, 1, 1)
        f2 = gather_copy(q, False, (y + 1) % 4, 1, 2, 5)
        f2.start()
        sends.extend((f1, f2))

    def gather_rest(q):
        gather_wait(q, 0, 1)
        gather_wait(q, 1, 0)
        gather_wait(q, 2, 0)
        gather_wait(q, 2, 1)

    def product(q, j, dst):
        s, r = CHUNKS[q]
        left = jnp.concatenate([abuf[(x + s) % 4, k, pl.ds(r * half, half), :] for k in range(8)], axis=1)
        total = jnp.dot(left, bbuf[j], preferred_element_type=jnp.float32)
        for i in range(2):
            dst[pl.ds(i, half, stride=2), :] = total[:, i * 128:(i + 1) * 128]

    def partial_copy(q, j):
        return remote(cp.at[q, j], cr.at[q, j], p_s.at[q, j], p_r.at[q, j], dev(x, c, y, buddy))

    def partial_send(q):
        @pl.loop(0, 2)
        def _(j):
            product(q, j, cp.at[q, j])
            partial_copy(q, j).start()

    def final_copy(q, j):
        s, r = CHUNKS[q]
        lines = pl.ds(r * 2 * half, 2 * half)
        h = x * 2 + par
        dst = out.at[h, lines]
        if s == 0 and j == 0:
            return pltpu.make_async_copy(cf.at[q, j], dst, o_s.at[q, j])
        return remote(cf.at[q, j], dst, o_s.at[q, j], o_r.at[h, r], dev((x + s) % 4, c, y, mir if j else z))

    def finish(q):
        @pl.loop(0, 2)
        def _(j):
            product(q, j + 2, cf.at[q, j])

        for j in (1, 0):
            partial_copy(q, j).wait_recv()
            cf[q, j] += cr[q, j]
            final_copy(q, j).start()

    a_start(0)
    b_start(0)
    b_start(1)
    a_start(1)
    a_start(2)
    gather_start(0)
    b_arrive(0)
    gather_forward(0)
    a_start(3)
    gather_start(1)
    b_arrive(1)
    for q in range(NQ):
        if q + 4 < NQ:
            a_start(q + 4)
        if q + 2 < NQ:
            gather_start(q + 2)
        if q == 0:
            b_start(2)
            b_start(3)
        if q + 1 < NQ:
            gather_forward(q + 1)
        gather_rest(q)
        partial_send(q)
        if q == LAG - 1:
            b_arrive(2)
            b_arrive(3)
        if q >= LAG:
            finish(q - LAG)
    for q in range(NQ - LAG, NQ):
        finish(q)

    for q in range(NQ):
        for j in range(2):
            partial_copy(q, j).wait_send()
            s, r = CHUNKS[q]
            if s == 0 and j == 0:
                final_copy(q, j).wait()
            else:
                final_copy(q, j).wait_send()
                h = (x + 4 - s) % 4 * 2 + (1 - par if j else par)
                dst = out.at[h, pl.ds(r * 2 * half, 2 * half)]
                remote(cf.at[q, j], dst, o_s.at[q, j], o_r.at[h, r], dev(x, c, y, mir)).wait_recv()
    for cp_ in sends:
        cp_.wait_send()
    b_wait_sends()
    b_forward_wait()


def per_device(amp, integrals, residual_in):
    irreps, blocks, blk, kb, _ = integrals.shape
    rows = blocks * blk
    left = integrals.reshape(irreps, rows, kb * blk)
    right = amp.reshape(kb * blk, 16, 2 * blk).transpose(1, 0, 2)
    dma = pltpu.SemaphoreType.DMA
    out = pl.pallas_call(
        kernel,
        out_shape=jax.ShapeDtypeStruct((irreps, rows * 2, blk), jnp.float32),
        in_specs=[pl.BlockSpec(memory_space=pl.ANY)] * 2,
        out_specs=pl.BlockSpec(memory_space=pl.ANY),
        scratch_shapes=[
            pltpu.VMEM((4, 8, rows, 256), jnp.bfloat16),
            pltpu.VMEM((4, 2048, 256), jnp.bfloat16),
            pltpu.VMEM((NQ, 2, rows, blk), jnp.float32),
            pltpu.VMEM((NQ, 2, rows, blk), jnp.float32),
            pltpu.VMEM((NQ, 2, rows, blk), jnp.float32),
            dma((4, 2, 2)), dma((4, 2, 2)),
            dma((NQ, 6)), dma((NQ, 3, 2)),
            dma((4, 4)), dma((4, 2, 4)), dma((4, 2, 4)),
            dma((NQ, 2)), dma((NQ, 2)),
            dma((NQ, 2)), dma((8, 2)),
        ],
        compiler_params=pltpu.CompilerParams(collective_id=0, has_side_effects=True, vmem_limit_bytes=60 << 20),
    )(left, right)
    return residual_in + out.reshape(residual_in.shape)


def solution(mesh):
    placed = (
        P("row", "col", None, None, None),
        P(None, "row", None, "col", None),
        P(None, "row", None, "col", None),
    )
    return jax.shard_map(
        per_device,
        mesh=mesh,
        in_specs=placed,
        out_specs=P(None, "row", None, "col", None),
        check_vma=False,
    )
```

```python
import jax
import jax.numpy as jnp
from jax import lax
from jax.experimental import pallas as pl
from jax.experimental.pallas import tpu as pltpu
from jax.sharding import PartitionSpec as P

MESH = pl.DeviceIdType.MESH
JXOR = (1, 2, 0, 3)
CHUNKS = (
    (0, 0, 192), (1, 0, 192), (1, 192, 192), (2, 0, 192), (2, 192, 192),
    (3, 0, 192), (3, 192, 192), (0, 192, 192),
)
NQ = len(CHUNKS)
BASE = tuple(2 * sum(n for _, _, n in CHUNKS[:q]) for q in range(NQ))
LINES = 2 * sum(n for _, _, n in CHUNKS)
PLAN = (
    "AS0", "BS1", "BL0", "BS0", "AS1", "GS0", "AS2", "BA1", "GF0", "AS3", "GS1", "BA0", "BL2", "BL3", "AS4",
    "GS2", "BS3", "BS2", "GF1", "GR0", "P0", "AS5", "GS3", "GF2", "GR1", "P1", "BA3", "BA2", "AS6", "GS4", "GF3",
    "GR2", "P2", "F0", "AS7", "GS5", "GF4", "GR3", "P3", "F1", "GS6", "GF5", "GR4", "P4", "F2", "GS7", "GF6",
    "GR5", "P5", "F3", "GF7", "GR6", "P6", "F4", "GR7", "P7", "F5", "O60", "O61", "O70", "O71", "W61", "W60",
    "W71", "W70",
)


def kernel(a_in, b_in, out, araw, braw, atmp, btmp, ast, bst, abuf, bbuf, cp, cr, cf,
           in_s, a_s, a_r, g_s, g_r, b_s, b_r, f_s, p_s, p_r, o_s, o_r):
    row, col = lax.axis_index("row"), lax.axis_index("col")
    x, c, y, z = row // 2, row % 2, col // 4, col % 4
    par = z // 2
    mir = 3 - z
    buddy = z + 1 - 2 * (z % 2)

    def dev(xx, cc, yy, zz):
        return (xx * 2 + cc, yy * 4 + zz)

    def xor(zz, j):
        lo, hi = zz % 2, zz // 2
        m = JXOR[j]
        lo = 1 - lo if m % 2 else lo
        hi = 1 - hi if m // 2 else hi
        return hi * 2 + lo

    def remote(src, dst, ss, rs, d):
        return pltpu.make_async_remote_copy(src, dst, ss, rs, device_id=d, device_id_type=MESH)

    b_load = pltpu.make_async_copy(b_in, braw, in_s.at[0])
    a_load = pltpu.make_async_copy(a_in, araw, in_s.at[1])
    b_load.start()
    a_load.start()
    barrier = pltpu.get_barrier_semaphore()
    peers = []
    for d in range(4):
        for zz in (z, mir):
            if d or zz is mir:
                peers.append(dev((x + d) % 4, c, y, zz))
            if d:
                peers.append(dev(x, c, (y + d) % 4, zz))
    peers.append(dev(x, 1 - c, y, z))
    peers.append(dev(x, c, y, buddy))
    for d in peers:
        pl.semaphore_signal(barrier, inc=1, device_id=d, device_id_type=MESH)
    b_load.wait()

    @pl.loop(0, 8)
    def _(t):
        ks = pl.ds(t * 32, 32)
        btmp[pl.ds(t * 1024, 1024), :] = braw[ks].astype(jnp.float32).reshape(1024, 128)

    def b_lay(j):
        zj = jnp.where(c == par, xor(z, j), xor(mir, j))
        for yd in range(4):
            for i in range(2):
                lines = btmp[pl.ds(yd * 8 + zj * 2 + i, 256, stride=32), :]
                bst[j, yd, :, i * 128:(i + 1) * 128] = lines.astype(jnp.bfloat16)

    def a_lay(q):
        dx, off, n = CHUNKS[q]
        hx = (x + 4 - dx) % 4
        for zz in range(2):
            h = hx * 2 + (1 - par if zz else par)
            atmp[pl.ds(0, 2 * n), :] = araw[h, pl.ds(2 * off, 2 * n), :].astype(jnp.float32)
            for i in range(2):
                lines = atmp[pl.ds(i, n, stride=2), :].astype(jnp.bfloat16)
                lanes = slice(i * 128, (i + 1) * 128)
                if dx == 0 and zz == 0:
                    abuf[x, y * 2, off:off + n, lanes] = lines
                else:
                    ast[h, off:off + n, lanes] = lines

    b_lay(1)
    a_load.wait()
    a_lay(0)
    pl.semaphore_wait(barrier, len(peers))

    sends = []

    def b_block(j, ys, zz):
        return bbuf.at[j, pl.ds(pl.multiple_of((ys * 2 + zz) * 256, 256), 256)]

    def b_start(j, dys=(1, 3, 2, 0)):
        for dy in dys:
            yd = (y + dy) % 4

            def go(zd, zz, local):
                src = bst.at[j, yd]
                dst = b_block(j, y, zz)
                if local:
                    pltpu.make_async_copy(src, dst, b_r.at[y, zz, j]).start()
                else:
                    remote(src, dst, b_s.at[dy, j], b_r.at[y, zz, j], dev(x, c, yd, zd)).start()

            @pl.when(c == par)
            def _():
                go(z, 0, dy == 0)

            @pl.when(c != par)
            def _():
                go(mir, 1, False)

    def b_wait_sends():
        for j in range(4):
            for dy in range(4):
                cp_ = remote(bst.at[0, 0], b_block(0, 0, 0), b_s.at[dy, j], b_r.at[0, 0, j], dev(x, c, y, mir))
                if dy == 0:
                    @pl.when(c != par)
                    def _():
                        cp_.wait_send()
                else:
                    cp_.wait_send()

    def b_arrive(j):
        for dy in (0, 1, 3, 2):
            ys = (y + dy) % 4
            for zz in range(2):
                blk = b_block(j, ys, zz)
                fw = remote(blk, blk, f_s.at[dy, zz, j], b_r.at[ys, zz, j], dev(x, 1 - c, y, z))
                fw.wait_recv()

                @pl.when(c == par)
                def _():
                    fw.start()

    def b_forward_wait():
        @pl.when(c == par)
        def _():
            for j in range(4):
                for dy in range(4):
                    for zz in range(2):
                        blk = b_block(j, 0, 0)
                        remote(blk, blk, f_s.at[dy, zz, j], b_r.at[0, zz, j], dev(x, 1 - c, y, z)).wait_send()

    def a_block(q, ys, zz):
        s, off, n = CHUNKS[q]
        return abuf.at[(x + s) % 4, ys * 2 + zz, pl.ds(off, n)]

    def a_start(q):
        dx, off, n = CHUNKS[q]
        hx = (x + 4 - dx) % 4
        if q:
            a_lay(q)
        for zz in (1, 0):
            if dx or zz:
                zd = mir if zz else z
                src = ast.at[hx * 2 + zd // 2, pl.ds(off, n)]
                dst = abuf.at[x, y * 2 + zz, pl.ds(off, n)]
                cp_ = remote(src, dst, a_s.at[q, zz], a_r.at[q, zz], dev(hx, c, y, zd))
                cp_.start()
                sends.append(cp_)

    def a_arrive(q, zz):
        if CHUNKS[q][0] or zz:
            blk = a_block(q, y, zz)
            remote(blk, blk, a_s.at[q, zz], a_r.at[q, zz], dev(x, c, y, mir)).wait_recv()

    def gather_copy(q, up, ys, zz, frm, k):
        blk = a_block(q, ys, zz)
        to = (y + 1) % 4 if up else (y + 3) % 4
        return remote(blk, blk, g_s.at[q, k], g_r.at[q, frm, zz], dev(x, c, to, z))

    def gather_start(q):
        for k, (up, zz) in enumerate(((True, 0), (False, 0), (False, 1), (True, 1))):
            if k == 0 or k == 2:
                a_arrive(q, zz)
            cp_ = gather_copy(q, up, y, zz, 0 if up else 1, k)
            cp_.start()
            sends.append(cp_)

    def gather_wait(q, frm, zz):
        blk = a_block(q, (y + (3, 1, 2)[frm]) % 4, zz)
        remote(blk, blk, g_s.at[q, 0], g_r.at[q, frm, zz], dev(x, c, y, mir)).wait_recv()

    def gather_forward(q):
        gather_wait(q, 0, 0)
        f1 = gather_copy(q, True, (y + 3) % 4, 0, 2, 4)
        f1.start()
        gather_wait(q, 1, 1)
        f2 = gather_copy(q, False, (y + 1) % 4, 1, 2, 5)
        f2.start()
        sends.extend((f1, f2))

    def gather_rest(q):
        gather_wait(q, 0, 1)
        gather_wait(q, 1, 0)
        gather_wait(q, 2, 0)
        gather_wait(q, 2, 1)

    def product(q, j, dst):
        s, off, n = CHUNKS[q]
        left = jnp.concatenate([abuf[(x + s) % 4, k, pl.ds(off, n), :] for k in range(8)], axis=1)
        total = jnp.dot(left, bbuf[j], preferred_element_type=jnp.float32)
        for i in range(2):
            dst[pl.ds(BASE[q] + i, n, stride=2), :] = total[:, i * 128:(i + 1) * 128]

    def lines_of(q):
        return pl.ds(BASE[q], 2 * CHUNKS[q][2])

    def partial_copy(q, j):
        return remote(cp.at[j, lines_of(q)], cr.at[j, lines_of(q)], p_s.at[q, j], p_r.at[q, j], dev(x, c, y, buddy))

    def partial_send(q, first=0, count=2):
        @pl.loop(first, first + count)
        def _(i):
            j = 1 - i
            product(q, j, cp.at[j])
            partial_copy(q, j).start()

    def final_copy(q, j):
        s, off, n = CHUNKS[q]
        src = cf.at[j, lines_of(q)]
        dst = out.at[x * 2 + par, pl.ds(2 * off, 2 * n)]
        if s == 0 and j == 0:
            return pltpu.make_async_copy(src, dst, o_s.at[q, j])
        return remote(src, dst, o_s.at[q, j], o_r.at[q, j], dev((x + s) % 4, c, y, mir if j else z))

    def final_arrive(q, j):
        s, off, n = CHUNKS[q]
        h = (x + 4 - s) % 4 * 2 + (1 - par if j else par)
        dst = out.at[h, pl.ds(2 * off, 2 * n)]
        remote(cf.at[j, lines_of(q)], dst, o_s.at[q, j], o_r.at[q, j], dev(x, c, y, mir)).wait_recv()

    def own(q, j):
        product(q, j + 2, cf.at[j])

    def finish(q, j):
        partial_copy(q, j).wait_recv()
        cf[j, lines_of(q), :] += cr[j, lines_of(q), :]
        final_copy(q, j).start()

    steps = dict(AS=a_start, BL=b_lay, BA=b_arrive, GS=gather_start, GF=gather_forward, GR=gather_rest)
    for step in PLAN:
        args = [int(d) for d in step if d.isdigit()]
        name = step.rstrip("0123456789")
        if name == "P":
            partial_send(args[0], *((1 - args[1], 1) if len(args) > 1 else ()))
        elif name == "BS":
            b_start(args[0], ((1, 3), (2, 0))[args[1]] if len(args) > 1 else (1, 3, 2, 0))
        elif name == "F":
            for j in args[1:] or (1, 0):
                own(args[0], j)
                finish(args[0], j)
        elif name == "O":
            own(*args)
        elif name == "W":
            finish(*args)
        else:
            steps[name](*args)

    for q in range(NQ):
        for j in range(2):
            partial_copy(q, j).wait_send()
            if CHUNKS[q][0] == 0 and j == 0:
                final_copy(q, j).wait()
            else:
                final_copy(q, j).wait_send()
                final_arrive(q, j)
    for cp_ in sends:
        cp_.wait_send()
    b_wait_sends()
    b_forward_wait()


def per_device(amp, integrals, residual_in):
    irreps, blocks, blk, kb, _ = integrals.shape
    rows = blocks * blk
    left = integrals.reshape(irreps, rows * kb, blk)
    right = amp.reshape(kb * blk, 32, blk)
    res = residual_in.reshape(irreps, rows * 2, blk)
    dma = pltpu.SemaphoreType.DMA
    out = pl.pallas_call(
        kernel,
        out_shape=jax.ShapeDtypeStruct(res.shape, jnp.float32),
        in_specs=[pl.BlockSpec(memory_space=pl.ANY)] * 2,
        out_specs=pl.BlockSpec(memory_space=pl.ANY),
        scratch_shapes=[
            pltpu.VMEM(left.shape, jnp.bfloat16),
            pltpu.VMEM(right.shape, jnp.bfloat16),
            pltpu.VMEM((384, blk), jnp.float32),
            pltpu.VMEM((8192, blk), jnp.float32),
            pltpu.VMEM((8, rows, 256), jnp.bfloat16),
            pltpu.VMEM((4, 4, 256, 256), jnp.bfloat16),
            pltpu.VMEM((4, 8, rows, 256), jnp.bfloat16),
            pltpu.VMEM((4, 2048, 256), jnp.bfloat16),
            pltpu.VMEM((2, LINES, blk), jnp.float32),
            pltpu.VMEM((2, LINES, blk), jnp.float32),
            pltpu.VMEM((2, LINES, blk), jnp.float32),
            dma((2,)),
            dma((NQ, 2)), dma((NQ, 2)),
            dma((NQ, 6)), dma((NQ, 3, 2)),
            dma((4, 4)), dma((4, 2, 4)), dma((4, 2, 4)),
            dma((NQ, 2)), dma((NQ, 2)),
            dma((NQ, 2)), dma((NQ, 2)),
        ],
        compiler_params=pltpu.CompilerParams(collective_id=0, has_side_effects=True, vmem_limit_bytes=60 << 20),
    )(left, right)
    return (res + out).reshape(residual_in.shape)


def solution(mesh):
    placed = (
        P("row", "col", None, None, None),
        P(None, "row", None, "col", None),
        P(None, "row", None, "col", None),
    )
    return jax.shard_map(
        per_device,
        mesh=mesh,
        in_specs=placed,
        out_specs=P(None, "row", None, "col", None),
        check_vma=False,
    )
```

```python
import jax
import jax.numpy as jnp
from jax import lax
from jax.experimental import pallas as pl
from jax.experimental.pallas import tpu as pltpu
from jax.sharding import PartitionSpec as P

MESH = pl.DeviceIdType.MESH
JXOR = (1, 2, 0, 3)
CHUNKS = (
    (0, 0, 192), (1, 0, 192), (1, 192, 192), (2, 0, 192), (2, 192, 192),
    (3, 0, 192), (3, 192, 192), (0, 192, 192),
)
NQ = len(CHUNKS)
BASE = tuple(2 * sum(n for _, _, n in CHUNKS[:q]) for q in range(NQ))
LINES = 2 * sum(n for _, _, n in CHUNKS)
PIECES = (4, 1, 1, 2)
PLAN = (
    "AS0", "BS1", "BL0", "BS0", "AS1", "GS0", "AS2", "BA1", "GF0", "AS3", "GS1", "BL2", "BL3", "GR0", "P01",
    "BA0", "AS4", "GS2", "GF1", "P00", "AS5", "GS3", "BS3", "BS2", "GF2", "GR1", "P1", "AS6", "GS4", "GF3", "GR2",
    "P2", "BA3", "BA2", "F01", "F00", "AS7", "GS5", "GF4", "GR3", "P3", "F11", "F10", "GS6", "GF5", "GR4", "P4",
    "F21", "F20", "GS7", "GF6", "GR5", "P5", "F31", "F30", "GF7", "GR6", "P6", "F41", "F40", "GR7", "P7", "F51",
    "F50", "O61", "O60", "O71", "O70", "Z", "W61", "W60", "W71", "W70",
)


def kernel(a_in, b_in, out, araw, braw, atmp, btmp, ast, bst, abuf, bbuf, cp, cr, cf,
           in_s, a_s, a_r, g_s, g_r, b_s, b_r, f_s, p_s, p_r, o_s, o_r):
    row, col = lax.axis_index("row"), lax.axis_index("col")
    x, c, y, z = row // 2, row % 2, col // 4, col % 4
    par = z // 2
    mir = 3 - z
    buddy = z + 1 - 2 * (z % 2)

    def dev(xx, cc, yy, zz):
        return (xx * 2 + cc, yy * 4 + zz)

    def xor(zz, j):
        lo, hi = zz % 2, zz // 2
        m = JXOR[j]
        lo = 1 - lo if m % 2 else lo
        hi = 1 - hi if m // 2 else hi
        return hi * 2 + lo

    def remote(src, dst, ss, rs, d):
        return pltpu.make_async_remote_copy(src, dst, ss, rs, device_id=d, device_id_type=MESH)

    b_load = pltpu.make_async_copy(b_in, braw, in_s.at[0])
    a_load = pltpu.make_async_copy(a_in, araw, in_s.at[1])
    b_load.start()
    a_load.start()
    barrier = pltpu.get_barrier_semaphore()
    peers = []
    for d in range(4):
        for zz in (z, mir):
            if d or zz is mir:
                peers.append(dev((x + d) % 4, c, y, zz))
            if d:
                peers.append(dev(x, c, (y + d) % 4, zz))
    peers.append(dev(x, 1 - c, y, z))
    peers.append(dev(x, c, y, buddy))
    for d in peers:
        pl.semaphore_signal(barrier, inc=1, device_id=d, device_id_type=MESH)
    b_load.wait()

    @pl.loop(0, 8)
    def _(t):
        ks = pl.ds(t * 32, 32)
        btmp[pl.ds(t * 1024, 1024), :] = braw[ks].astype(jnp.float32).reshape(1024, 128)

    def b_lay(j):
        zj = jnp.where(c == par, xor(z, j), xor(mir, j))
        for yd in range(4):
            for i in range(2):
                lines = btmp[pl.ds(yd * 8 + zj * 2 + i, 256, stride=32), :]
                bst[j, yd, :, i * 128:(i + 1) * 128] = lines.astype(jnp.bfloat16)

    def a_lay(q):
        dx, off, n = CHUNKS[q]
        hx = (x + 4 - dx) % 4
        for zz in range(2):
            h = hx * 2 + (1 - par if zz else par)
            atmp[pl.ds(0, 2 * n), :] = araw[h, pl.ds(2 * off, 2 * n), :].astype(jnp.float32)
            for i in range(2):
                lines = atmp[pl.ds(i, n, stride=2), :].astype(jnp.bfloat16)
                lanes = slice(i * 128, (i + 1) * 128)
                if dx == 0 and zz == 0:
                    abuf[x, y * 2, off:off + n, lanes] = lines
                else:
                    ast[h, off:off + n, lanes] = lines

    b_lay(1)
    a_load.wait()
    a_lay(0)
    pl.semaphore_wait(barrier, len(peers))

    sends = []

    def start(blocks, pieces):
        src, dst, off, n, ss, rs, d = blocks
        for k in range(pieces):
            rows = pl.ds(off + k * (n // pieces), n // pieces)
            remote(src.at[rows], dst.at[rows], ss, rs, d).start()
        rows = pl.ds(off, n)
        sends.append(remote(src.at[rows], dst.at[rows], ss, rs, d))

    def b_block(j, ys, zz):
        return bbuf.at[j, pl.ds(pl.multiple_of((ys * 2 + zz) * 256, 256), 256)]

    def b_start(j, dys=(1, 3, 2, 0)):
        for dy in dys:
            yd = (y + dy) % 4

            def go(zd, zz, local):
                src = bst.at[j, yd]
                dst = b_block(j, y, zz)
                if local:
                    pltpu.make_async_copy(src, dst, b_r.at[y, zz, j]).start()
                else:
                    remote(src, dst, b_s.at[dy, j], b_r.at[y, zz, j], dev(x, c, yd, zd)).start()

            @pl.when(c == par)
            def _():
                go(z, 0, dy == 0)

            @pl.when(c != par)
            def _():
                go(mir, 1, False)

    def b_wait_sends():
        for j in range(4):
            for dy in range(4):
                cp_ = remote(bst.at[0, 0], b_block(0, 0, 0), b_s.at[dy, j], b_r.at[0, 0, j], dev(x, c, y, mir))
                if dy == 0:
                    @pl.when(c != par)
                    def _():
                        cp_.wait_send()
                else:
                    cp_.wait_send()

    def b_pair(j, dy):
        ys = (y + dy) % 4
        blk = bbuf.at[j, pl.ds(pl.multiple_of(ys * 512, 512), 512)]
        return remote(blk, blk, f_s.at[dy, j], b_r.at[ys, 0, j], dev(x, 1 - c, y, z))

    def b_arrive(j):
        for dy in (0, 1, 3, 2):
            ys = (y + dy) % 4

            @pl.when(c == par)
            def _():
                for zz in range(2):
                    blk = b_block(j, ys, zz)
                    remote(blk, blk, f_s.at[dy, j], b_r.at[ys, zz, j], dev(x, 1 - c, y, z)).wait_recv()
                b_pair(j, dy).start()

            @pl.when(c != par)
            def _():
                b_pair(j, dy).wait_recv()

    def b_forward_wait():
        @pl.when(c == par)
        def _():
            for j in range(4):
                for dy in range(4):
                    b_pair(j, dy).wait_send()

    def a_block(q, ys, zz):
        s, off, n = CHUNKS[q]
        return abuf.at[(x + s) % 4, ys * 2 + zz, pl.ds(off, n)]

    def a_start(q):
        dx, off, n = CHUNKS[q]
        hx = (x + 4 - dx) % 4
        if q:
            a_lay(q)
        for zz in (1, 0):
            if dx or zz:
                zd = mir if zz else z
                start((ast.at[hx * 2 + zd // 2], abuf.at[x, y * 2 + zz], off, n,
                       a_s.at[q, zz], a_r.at[q, zz], dev(hx, c, y, zd)), PIECES[0] if q == 0 else PIECES[1])

    def a_arrive(q, zz):
        if CHUNKS[q][0] or zz:
            blk = a_block(q, y, zz)
            remote(blk, blk, a_s.at[q, zz], a_r.at[q, zz], dev(x, c, y, mir)).wait_recv()

    def gather_copy(q, up, ys, zz, frm, k, pieces):
        s, off, n = CHUNKS[q]
        blk = abuf.at[(x + s) % 4, ys * 2 + zz]
        to = (y + 1) % 4 if up else (y + 3) % 4
        start((blk, blk, off, n, g_s.at[q, k], g_r.at[q, frm, zz], dev(x, c, to, z)), pieces)

    def gather_start(q):
        for k, (up, zz) in enumerate(((True, 0), (False, 0), (False, 1), (True, 1))):
            if k == 0 or k == 2:
                a_arrive(q, zz)
            gather_copy(q, up, y, zz, 0 if up else 1, k, PIECES[2])

    def gather_wait(q, frm, zz):
        blk = a_block(q, (y + (3, 1, 2)[frm]) % 4, zz)
        remote(blk, blk, g_s.at[q, 0], g_r.at[q, frm, zz], dev(x, c, y, mir)).wait_recv()

    def gather_forward(q):
        gather_wait(q, 0, 0)
        gather_copy(q, True, (y + 3) % 4, 0, 2, 4, PIECES[3])
        gather_wait(q, 1, 1)
        gather_copy(q, False, (y + 1) % 4, 1, 2, 5, PIECES[3])

    def gather_rest(q):
        gather_wait(q, 0, 1)
        gather_wait(q, 1, 0)
        gather_wait(q, 2, 0)
        gather_wait(q, 2, 1)

    def product(q, j, dst, more=None):
        s, off, n = CHUNKS[q]
        left = jnp.concatenate([abuf[(x + s) % 4, k, pl.ds(off, n), :] for k in range(8)], axis=1)
        total = jnp.dot(left, bbuf[j], preferred_element_type=jnp.float32)
        for i in range(2):
            lines = pl.ds(BASE[q] + i, n, stride=2)
            part = total[:, i * 128:(i + 1) * 128]
            dst[lines, :] = part if more is None else part + more[lines, :]

    def lines_of(q):
        return pl.ds(BASE[q], 2 * CHUNKS[q][2])

    def partial_copy(q, j):
        return remote(cp.at[j, lines_of(q)], cr.at[j, lines_of(q)], p_s.at[q, j], p_r.at[q, j], dev(x, c, y, buddy))

    def partial_send(q, first=0, count=2):
        @pl.loop(first, first + count)
        def _(i):
            j = 1 - i
            product(q, j, cp.at[j])
            partial_copy(q, j).start()

    def final_copy(q, j):
        s, off, n = CHUNKS[q]
        src = cf.at[j, lines_of(q)]
        dst = out.at[x * 2 + par, pl.ds(2 * off, 2 * n)]
        if s == 0 and j == 0:
            return pltpu.make_async_copy(src, dst, o_s.at[q, j])
        return remote(src, dst, o_s.at[q, j], o_r.at[q, j], dev((x + s) % 4, c, y, mir if j else z))

    def final_arrive(q, j):
        s, off, n = CHUNKS[q]
        h = (x + 4 - s) % 4 * 2 + (1 - par if j else par)
        dst = out.at[h, pl.ds(2 * off, 2 * n)]
        remote(cf.at[j, lines_of(q)], dst, o_s.at[q, j], o_r.at[q, j], dev(x, c, y, mir)).wait_recv()

    def own(q, j):
        product(q, j + 2, cf.at[j])

    def finish(q, j):
        partial_copy(q, j).wait_recv()
        cf[j, lines_of(q), :] += cr[j, lines_of(q), :]
        final_copy(q, j).start()

    steps = dict(AS=a_start, BL=b_lay, BA=b_arrive, GS=gather_start, GF=gather_forward, GR=gather_rest)
    for step in PLAN:
        args = [int(d) for d in step if d.isdigit()]
        name = step.rstrip("0123456789")
        if name == "P":
            partial_send(args[0], *((1 - args[1], 1) if len(args) > 1 else ()))
        elif name == "BS":
            b_start(args[0], ((1, 3), (2, 0))[args[1]] if len(args) > 1 else (1, 3, 2, 0))
        elif name == "F":
            for j in args[1:] or (1, 0):
                partial_copy(args[0], j).wait_recv()
                product(args[0], j + 2, cf.at[j], cr.at[j])
                final_copy(args[0], j).start()
        elif name == "Z":
            for cp_ in sends:
                cp_.wait_send()
            b_wait_sends()
            b_forward_wait()
        elif name == "O":
            own(*args)
        elif name == "W":
            finish(*args)
        else:
            steps[name](*args)

    for q in range(NQ):
        for j in range(2):
            partial_copy(q, j).wait_send()
            if CHUNKS[q][0] == 0 and j == 0:
                final_copy(q, j).wait()
            else:
                final_copy(q, j).wait_send()
                final_arrive(q, j)

def per_device(amp, integrals, residual_in):
    irreps, blocks, blk, kb, _ = integrals.shape
    rows = blocks * blk
    left = integrals.reshape(irreps, rows * kb, blk)
    right = amp.reshape(kb * blk, 32, blk)
    res = residual_in.reshape(irreps, rows * 2, blk)
    dma = pltpu.SemaphoreType.DMA
    out = pl.pallas_call(
        kernel,
        out_shape=jax.ShapeDtypeStruct(res.shape, jnp.float32),
        in_specs=[pl.BlockSpec(memory_space=pl.ANY)] * 2,
        out_specs=pl.BlockSpec(memory_space=pl.ANY),
        scratch_shapes=[
            pltpu.VMEM(left.shape, jnp.bfloat16),
            pltpu.VMEM(right.shape, jnp.bfloat16),
            pltpu.VMEM((384, blk), jnp.float32),
            pltpu.VMEM((8192, blk), jnp.float32),
            pltpu.VMEM((8, rows, 256), jnp.bfloat16),
            pltpu.VMEM((4, 4, 256, 256), jnp.bfloat16),
            pltpu.VMEM((4, 8, rows, 256), jnp.bfloat16),
            pltpu.VMEM((4, 2048, 256), jnp.bfloat16),
            pltpu.VMEM((2, LINES, blk), jnp.float32),
            pltpu.VMEM((2, LINES, blk), jnp.float32),
            pltpu.VMEM((2, LINES, blk), jnp.float32),
            dma((2,)),
            dma((NQ, 2)), dma((NQ, 2)),
            dma((NQ, 6)), dma((NQ, 3, 2)),
            dma((4, 4)), dma((4, 2, 4)), dma((4, 4)),
            dma((NQ, 2)), dma((NQ, 2)),
            dma((NQ, 2)), dma((NQ, 2)),
        ],
        compiler_params=pltpu.CompilerParams(collective_id=0, has_side_effects=True, vmem_limit_bytes=60 << 20),
    )(left, right)
    return (res + out).reshape(residual_in.shape)


def solution(mesh):
    placed = (
        P("row", "col", None, None, None),
        P(None, "row", None, "col", None),
        P(None, "row", None, "col", None),
    )
    return jax.shard_map(
        per_device,
        mesh=mesh,
        in_specs=placed,
        out_specs=P(None, "row", None, "col", None),
        check_vma=False,
    )
```

```python
import jax
import jax.numpy as jnp
from jax import lax
from jax.experimental import pallas as pl
from jax.experimental.pallas import tpu as pltpu
from jax.sharding import PartitionSpec as P

MESH = pl.DeviceIdType.MESH
JXOR = (1, 2, 0, 3)
CHUNKS = (
    (0, 0, 192), (1, 0, 192), (1, 192, 192), (2, 0, 192), (2, 192, 192),
    (3, 0, 192), (3, 192, 192), (0, 192, 192),
)
NQ = len(CHUNKS)
BASE = tuple(2 * sum(n for _, _, n in CHUNKS[:q]) for q in range(NQ))
LINES = 2 * sum(n for _, _, n in CHUNKS)
PIECES = (4, 1, 1, 2)
PLAN = (
    "AS0", "BS1", "BL0", "BS0", "AS1", "GS0", "AS2", "BA1", "GF0", "AS3", "GS1", "BL2", "BL3", "GR0", "P01",
    "BA0", "AS4", "GS2", "GF1", "P00", "AS5", "GS3", "BS3", "BS2", "GF2", "GR1", "P1", "AS6", "GS4", "GF3", "GR2",
    "P2", "BA3", "BA2", "F01", "F00", "AS7", "GS5", "GF4", "GR3", "P3", "F11", "F10", "GS6", "GF5", "GR4", "P4",
    "F21", "F20", "GS7", "GF6", "GR5", "P5", "F31", "F30", "GF7", "GR6", "P6", "F41", "F40", "GR7", "P7", "F51",
    "F50", "O61", "O60", "O71", "O70", "Z", "W61", "W60", "W71", "W70",
)


def kernel(a_in, b_in, out, araw, braw, atmp, btmp, ast, bst, abuf, bbuf, cp, cr, cf,
           in_s, a_s, a_r, g_s, g_r, b_s, b_r, f_s, p_s, p_r, o_s, o_r):
    row, col = lax.axis_index("row"), lax.axis_index("col")
    x, c, y, z = row // 2, row % 2, col // 4, col % 4
    par = z // 2
    mir = 3 - z
    buddy = z + 1 - 2 * (z % 2)

    def dev(xx, cc, yy, zz):
        return (xx * 2 + cc, yy * 4 + zz)

    def xor(zz, j):
        lo, hi = zz % 2, zz // 2
        m = JXOR[j]
        lo = 1 - lo if m % 2 else lo
        hi = 1 - hi if m // 2 else hi
        return hi * 2 + lo

    def remote(src, dst, ss, rs, d):
        return pltpu.make_async_remote_copy(src, dst, ss, rs, device_id=d, device_id_type=MESH)

    b_load = pltpu.make_async_copy(b_in, braw, in_s.at[0])
    a_load = pltpu.make_async_copy(a_in, araw, in_s.at[1])
    b_load.start()
    a_load.start()
    barrier = pltpu.get_barrier_semaphore()
    peers = []
    for d in range(4):
        for zz in (z, mir):
            if d or zz is mir:
                peers.append(dev((x + d) % 4, c, y, zz))
            if d:
                peers.append(dev(x, c, (y + d) % 4, zz))
    peers.append(dev(x, 1 - c, y, z))
    peers.append(dev(x, c, y, buddy))
    for d in peers:
        pl.semaphore_signal(barrier, inc=1, device_id=d, device_id_type=MESH)
    b_load.wait()

    @pl.loop(0, 8)
    def _(t):
        ks = pl.ds(t * 32, 32)
        btmp[pl.ds(t * 1024, 1024), :] = braw[ks].astype(jnp.float32).reshape(1024, 128)

    def b_lay(j):
        zj = jnp.where(c == par, xor(z, j), xor(mir, j))
        for yd in range(4):
            for i in range(2):
                lines = btmp[pl.ds(yd * 8 + zj * 2 + i, 256, stride=32), :]
                bst[j, yd, :, i * 128:(i + 1) * 128] = lines.astype(jnp.bfloat16)

    def a_lay(q):
        dx, off, n = CHUNKS[q]
        hx = (x + 4 - dx) % 4
        for zz in range(2):
            h = hx * 2 + (1 - par if zz else par)
            atmp[pl.ds(0, 2 * n), :] = araw[h, pl.ds(2 * off, 2 * n), :].astype(jnp.float32)
            for i in range(2):
                lines = atmp[pl.ds(i, n, stride=2), :].astype(jnp.bfloat16)
                lanes = slice(i * 128, (i + 1) * 128)
                if dx == 0 and zz == 0:
                    abuf[x, y * 2, off:off + n, lanes] = lines
                else:
                    ast[h, off:off + n, lanes] = lines

    b_lay(1)
    a_load.wait()
    a_lay(0)
    pl.semaphore_wait(barrier, len(peers))

    sends = []

    def start(blocks, pieces):
        src, dst, off, n, ss, rs, d = blocks
        for k in range(pieces):
            rows = pl.ds(off + k * (n // pieces), n // pieces)
            remote(src.at[rows], dst.at[rows], ss, rs, d).start()
        rows = pl.ds(off, n)
        sends.append(remote(src.at[rows], dst.at[rows], ss, rs, d))

    def b_block(j, ys, zz):
        return bbuf.at[j, pl.ds(pl.multiple_of((ys * 2 + zz) * 256, 256), 256)]

    def b_start(j, dys=(1, 3, 2, 0)):
        for dy in dys:
            yd = (y + dy) % 4

            def go(zd, zz, local):
                src = bst.at[j, yd]
                dst = b_block(j, y, zz)
                if local:
                    pltpu.make_async_copy(src, dst, b_r.at[y, zz, j]).start()
                else:
                    remote(src, dst, b_s.at[dy, j], b_r.at[y, zz, j], dev(x, c, yd, zd)).start()

            @pl.when(c == par)
            def _():
                go(z, 0, dy == 0)

            @pl.when(c != par)
            def _():
                go(mir, 1, False)

    def b_wait_sends():
        for j in range(4):
            for dy in range(4):
                cp_ = remote(bst.at[0, 0], b_block(0, 0, 0), b_s.at[dy, j], b_r.at[0, 0, j], dev(x, c, y, mir))
                if dy == 0:
                    @pl.when(c != par)
                    def _():
                        cp_.wait_send()
                else:
                    cp_.wait_send()

    def b_pair(j, dy):
        ys = (y + dy) % 4
        blk = bbuf.at[j, pl.ds(pl.multiple_of(ys * 512, 512), 512)]
        return remote(blk, blk, f_s.at[dy, j], b_r.at[ys, 0, j], dev(x, 1 - c, y, z))

    def b_arrive(j):
        for dy in (0, 1, 3, 2):
            ys = (y + dy) % 4

            @pl.when(c == par)
            def _():
                for zz in range(2):
                    blk = b_block(j, ys, zz)
                    remote(blk, blk, f_s.at[dy, j], b_r.at[ys, zz, j], dev(x, 1 - c, y, z)).wait_recv()
                b_pair(j, dy).start()

            @pl.when(c != par)
            def _():
                b_pair(j, dy).wait_recv()

    def b_forward_wait():
        @pl.when(c == par)
        def _():
            for j in range(4):
                for dy in range(4):
                    b_pair(j, dy).wait_send()

    def a_block(q, ys, zz):
        s, off, n = CHUNKS[q]
        return abuf.at[(x + s) % 4, ys * 2 + zz, pl.ds(off, n)]

    def a_start(q):
        dx, off, n = CHUNKS[q]
        hx = (x + 4 - dx) % 4
        if q:
            a_lay(q)
        for zz in (1, 0):
            if dx or zz:
                zd = mir if zz else z
                start((ast.at[hx * 2 + zd // 2], abuf.at[x, y * 2 + zz], off, n,
                       a_s.at[q, zz], a_r.at[q, zz], dev(hx, c, y, zd)), PIECES[0] if q == 0 else PIECES[1])

    def a_arrive(q, zz):
        if CHUNKS[q][0] or zz:
            blk = a_block(q, y, zz)
            remote(blk, blk, a_s.at[q, zz], a_r.at[q, zz], dev(x, c, y, mir)).wait_recv()

    def gather_copy(q, up, ys, zz, frm, k, pieces):
        s, off, n = CHUNKS[q]
        blk = abuf.at[(x + s) % 4, ys * 2 + zz]
        to = (y + 1) % 4 if up else (y + 3) % 4
        start((blk, blk, off, n, g_s.at[q, k], g_r.at[q, frm, zz], dev(x, c, to, z)), pieces)

    def gather_start(q):
        for k, (up, zz) in enumerate(((True, 0), (False, 0), (False, 1), (True, 1))):
            if k == 0 or k == 2:
                a_arrive(q, zz)
            gather_copy(q, up, y, zz, 0 if up else 1, k, PIECES[2])

    def gather_wait(q, frm, zz):
        blk = a_block(q, (y + (3, 1, 2)[frm]) % 4, zz)
        remote(blk, blk, g_s.at[q, 0], g_r.at[q, frm, zz], dev(x, c, y, mir)).wait_recv()

    def gather_forward(q):
        gather_wait(q, 0, 0)
        gather_copy(q, True, (y + 3) % 4, 0, 2, 4, PIECES[3])
        gather_wait(q, 1, 1)
        gather_copy(q, False, (y + 1) % 4, 1, 2, 5, PIECES[3])

    def gather_rest(q):
        gather_wait(q, 0, 1)
        gather_wait(q, 1, 0)
        gather_wait(q, 2, 0)
        gather_wait(q, 2, 1)

    def product(q, j, dst, more=None):
        s, off, n = CHUNKS[q]
        left = jnp.concatenate([abuf[(x + s) % 4, k, pl.ds(off, n), :] for k in range(8)], axis=1)
        total = jnp.dot(left, bbuf[j], preferred_element_type=jnp.float32)
        for i in range(2):
            lines = pl.ds(BASE[q] + i, n, stride=2)
            part = total[:, i * 128:(i + 1) * 128]
            dst[lines, :] = part if more is None else part + more[lines, :]

    def lines_of(q):
        return pl.ds(BASE[q], 2 * CHUNKS[q][2])

    def partial_copy(q, j):
        return remote(cp.at[j, lines_of(q)], cr.at[j, lines_of(q)], p_s.at[q, j], p_r.at[q, j], dev(x, c, y, buddy))

    def partial_send(q, first=0, count=2):
        @pl.loop(first, first + count)
        def _(i):
            j = 1 - i
            product(q, j, cp.at[j])
            partial_copy(q, j).start()

    def final_copy(q, j):
        s, off, n = CHUNKS[q]
        src = cf.at[j, lines_of(q)]
        dst = out.at[x * 2 + par, pl.ds(2 * off, 2 * n)]
        if s == 0 and j == 0:
            return pltpu.make_async_copy(src, dst, o_s.at[q, j])
        return remote(src, dst, o_s.at[q, j], o_r.at[q, j], dev((x + s) % 4, c, y, mir if j else z))

    def final_arrive(q, j):
        s, off, n = CHUNKS[q]
        h = (x + 4 - s) % 4 * 2 + (1 - par if j else par)
        dst = out.at[h, pl.ds(2 * off, 2 * n)]
        remote(cf.at[j, lines_of(q)], dst, o_s.at[q, j], o_r.at[q, j], dev(x, c, y, mir)).wait_recv()

    def own(q, j):
        product(q, j + 2, cf.at[j])

    def finish(q, j):
        partial_copy(q, j).wait_recv()
        cf[j, lines_of(q), :] += cr[j, lines_of(q), :]
        final_copy(q, j).start()

    steps = dict(AS=a_start, BL=b_lay, BA=b_arrive, GS=gather_start, GF=gather_forward, GR=gather_rest)
    for step in PLAN:
        args = [int(d) for d in step if d.isdigit()]
        name = step.rstrip("0123456789")
        if name == "P":
            partial_send(args[0], *((1 - args[1], 1) if len(args) > 1 else ()))
        elif name == "BS":
            b_start(args[0], ((1, 3), (2, 0))[args[1]] if len(args) > 1 else (1, 3, 2, 0))
        elif name == "F":
            for j in args[1:] or (1, 0):
                partial_copy(args[0], j).wait_recv()
                product(args[0], j + 2, cf.at[j], cr.at[j])
                final_copy(args[0], j).start()
        elif name == "Z":
            for cp_ in sends:
                cp_.wait_send()
            b_wait_sends()
            b_forward_wait()
        elif name == "O":
            own(*args)
        elif name == "W":
            finish(*args)
        else:
            steps[name](*args)

    for q in range(NQ):
        for j in range(2):
            partial_copy(q, j).wait_send()
            if CHUNKS[q][0] == 0 and j == 0:
                final_copy(q, j).wait()
            else:
                final_copy(q, j).wait_send()
                final_arrive(q, j)

def per_device(amp, integrals, residual_in):
    irreps, blocks, blk, kb, _ = integrals.shape
    rows = blocks * blk
    left = integrals.reshape(irreps, rows * kb, blk)
    right = amp.reshape(kb * blk, 32, blk)
    res = residual_in.reshape(irreps, rows * 2, blk)
    dma = pltpu.SemaphoreType.DMA
    out = pl.pallas_call(
        kernel,
        out_shape=jax.ShapeDtypeStruct(res.shape, jnp.float32),
        in_specs=[pl.BlockSpec(memory_space=pl.ANY)] * 2,
        out_specs=pl.BlockSpec(memory_space=pl.ANY),
        scratch_shapes=[
            pltpu.VMEM(left.shape, jnp.bfloat16),
            pltpu.VMEM(right.shape, jnp.bfloat16),
            pltpu.VMEM((384, blk), jnp.float32),
            pltpu.VMEM((8192, blk), jnp.float32),
            pltpu.VMEM((8, rows, 256), jnp.bfloat16),
            pltpu.VMEM((4, 4, 256, 256), jnp.bfloat16),
            pltpu.VMEM((4, 8, rows, 256), jnp.bfloat16),
            pltpu.VMEM((4, 2048, 256), jnp.bfloat16),
            pltpu.VMEM((2, LINES, blk), jnp.float32),
            pltpu.VMEM((2, LINES, blk), jnp.float32),
            pltpu.VMEM((2, LINES, blk), jnp.float32),
            dma((2,)),
            dma((NQ, 2)), dma((NQ, 2)),
            dma((NQ, 6)), dma((NQ, 3, 2)),
            dma((4, 4)), dma((4, 2, 4)), dma((4, 4)),
            dma((NQ, 2)), dma((NQ, 2)),
            dma((NQ, 2)), dma((NQ, 2)),
        ],
        compiler_params=pltpu.CompilerParams(collective_id=0, has_side_effects=True, vmem_limit_bytes=36 << 20),
    )(left, right)
    return (res + out).reshape(residual_in.shape)


def solution(mesh):
    placed = (
        P("row", "col", None, None, None),
        P(None, "row", None, "col", None),
        P(None, "row", None, "col", None),
    )
    return jax.shard_map(
        per_device,
        mesh=mesh,
        in_specs=placed,
        out_specs=P(None, "row", None, "col", None),
        check_vma=False,
    )
```

```python
import jax
import jax.numpy as jnp
from jax import lax
from jax.experimental import pallas as pl
from jax.experimental.pallas import tpu as pltpu
from jax.sharding import PartitionSpec as P

MESH = pl.DeviceIdType.MESH
JXOR = (1, 2, 0, 3)
CHUNKS = (
    (0, 0, 192), (1, 0, 192), (1, 192, 192), (2, 0, 192), (2, 192, 192),
    (3, 0, 192), (3, 192, 192), (0, 192, 192),
)
NQ = len(CHUNKS)
BASE = tuple(2 * sum(n for _, _, n in CHUNKS[:q]) for q in range(NQ))
LINES = 2 * sum(n for _, _, n in CHUNKS)
PIECES = (4, 1, 1, 2)
PLAN = (
    "AS0", "BS1", "BL0", "BS0", "AS1", "GS0", "AS2", "BA1", "GF0", "AS3", "GS1", "BL2", "BL3", "GR0", "P01",
    "BA0", "AS4", "GS2", "GF1", "P00", "AS5", "GS3", "BS3", "BS2", "GF2", "GR1", "P1", "AS6", "GS4", "GF3", "GR2",
    "P2", "BA3", "BA2", "F01", "F00", "AS7", "GS5", "GF4", "GR3", "P3", "F11", "F10", "GS6", "GF5", "GR4", "P4",
    "F21", "F20", "GS7", "GF6", "GR5", "P5", "F31", "F30", "GF7", "GR6", "P6", "F41", "F40", "GR7", "P7", "F51",
    "F50", "O61", "O60", "O71", "O70", "Z", "W61", "W60", "W71", "W70",
)


def kernel(a_in, b_in, out, araw, braw, atmp, btmp, ast, bst, abuf, bbuf, cp, cr, cf,
           in_s, a_s, a_r, g_s, g_r, b_s, b_r, f_s, p_s, p_r, o_s, o_r):
    row, col = lax.axis_index("row"), lax.axis_index("col")
    x, c, y, z = row // 2, row % 2, col // 4, col % 4
    par = z // 2
    mir = 3 - z
    buddy = z + 1 - 2 * (z % 2)

    def dev(xx, cc, yy, zz):
        return (xx * 2 + cc, yy * 4 + zz)

    def xor(zz, j):
        lo, hi = zz % 2, zz // 2
        m = JXOR[j]
        lo = 1 - lo if m % 2 else lo
        hi = 1 - hi if m // 2 else hi
        return hi * 2 + lo

    def remote(src, dst, ss, rs, d):
        return pltpu.make_async_remote_copy(src, dst, ss, rs, device_id=d, device_id_type=MESH)

    b_load = pltpu.make_async_copy(b_in, braw, in_s.at[0])
    a_load = pltpu.make_async_copy(a_in, araw, in_s.at[1])
    b_load.start()
    a_load.start()
    barrier = pltpu.get_barrier_semaphore()
    peers = []
    for d in range(4):
        for zz in (z, mir):
            if d or zz is mir:
                peers.append(dev((x + d) % 4, c, y, zz))
            if d:
                peers.append(dev(x, c, (y + d) % 4, zz))
    peers.append(dev(x, 1 - c, y, z))
    peers.append(dev(x, c, y, buddy))
    for d in peers:
        pl.semaphore_signal(barrier, inc=1, device_id=d, device_id_type=MESH)
    b_load.wait()

    @pl.loop(0, 8)
    def _(t):
        ks = pl.ds(t * 32, 32)
        btmp[pl.ds(t * 1024, 1024), :] = braw[ks].astype(jnp.float32).reshape(1024, 128)

    def b_lay(j):
        zj = jnp.where(c == par, xor(z, j), xor(mir, j))
        for yd in range(4):
            for i in range(2):
                lines = btmp[pl.ds(yd * 8 + zj * 2 + i, 256, stride=32), :]
                bst[j, yd, :, i * 128:(i + 1) * 128] = lines.astype(jnp.bfloat16)

    def a_lay(q):
        dx, off, n = CHUNKS[q]
        hx = (x + 4 - dx) % 4
        for zz in range(2):
            h = hx * 2 + (1 - par if zz else par)
            atmp[pl.ds(0, 2 * n), :] = araw[h, pl.ds(2 * off, 2 * n), :].astype(jnp.float32)
            for i in range(2):
                lines = atmp[pl.ds(i, n, stride=2), :].astype(jnp.bfloat16)
                lanes = slice(i * 128, (i + 1) * 128)
                if dx == 0 and zz == 0:
                    abuf[x, y * 2, off:off + n, lanes] = lines
                else:
                    ast[h, off:off + n, lanes] = lines

    b_lay(1)
    a_load.wait()
    a_lay(0)
    pl.semaphore_wait(barrier, len(peers))

    sends = []

    def start(blocks, pieces):
        src, dst, off, n, ss, rs, d = blocks
        for k in range(pieces):
            rows = pl.ds(off + k * (n // pieces), n // pieces)
            remote(src.at[rows], dst.at[rows], ss, rs, d).start()
        rows = pl.ds(off, n)
        sends.append(remote(src.at[rows], dst.at[rows], ss, rs, d))

    def b_block(j, ys, zz):
        return bbuf.at[j, pl.ds(pl.multiple_of((ys * 2 + zz) * 256, 256), 256)]

    def b_start(j, dys=(1, 3, 2, 0)):
        for dy in dys:
            yd = (y + dy) % 4

            def go(zd, zz, local):
                src = bst.at[j, yd]
                dst = b_block(j, y, zz)
                if local:
                    pltpu.make_async_copy(src, dst, b_r.at[y, zz, j]).start()
                else:
                    remote(src, dst, b_s.at[dy, j], b_r.at[y, zz, j], dev(x, c, yd, zd)).start()

            @pl.when(c == par)
            def _():
                go(z, 0, dy == 0)

            @pl.when(c != par)
            def _():
                go(mir, 1, False)

    def b_wait_sends():
        for j in range(4):
            for dy in range(4):
                cp_ = remote(bst.at[0, 0], b_block(0, 0, 0), b_s.at[dy, j], b_r.at[0, 0, j], dev(x, c, y, mir))
                if dy == 0:
                    @pl.when(c != par)
                    def _():
                        cp_.wait_send()
                else:
                    cp_.wait_send()

    def b_pair(j, dy):
        ys = (y + dy) % 4
        blk = bbuf.at[j, pl.ds(pl.multiple_of(ys * 512, 512), 512)]
        return remote(blk, blk, f_s.at[dy, j], b_r.at[ys, 0, j], dev(x, 1 - c, y, z))

    def b_arrive(j):
        for dy in (0, 1, 3, 2):
            ys = (y + dy) % 4

            @pl.when(c == par)
            def _():
                for zz in range(2):
                    blk = b_block(j, ys, zz)
                    remote(blk, blk, f_s.at[dy, j], b_r.at[ys, zz, j], dev(x, 1 - c, y, z)).wait_recv()
                b_pair(j, dy).start()

            @pl.when(c != par)
            def _():
                b_pair(j, dy).wait_recv()

    def b_forward_wait():
        @pl.when(c == par)
        def _():
            for j in range(4):
                for dy in range(4):
                    b_pair(j, dy).wait_send()

    def a_block(q, ys, zz):
        s, off, n = CHUNKS[q]
        return abuf.at[(x + s) % 4, ys * 2 + zz, pl.ds(off, n)]

    def a_start(q):
        dx, off, n = CHUNKS[q]
        hx = (x + 4 - dx) % 4
        if q:
            a_lay(q)
        for zz in (1, 0):
            if dx or zz:
                zd = mir if zz else z
                start((ast.at[hx * 2 + zd // 2], abuf.at[x, y * 2 + zz], off, n,
                       a_s.at[q, zz], a_r.at[q, zz], dev(hx, c, y, zd)), PIECES[0] if q == 0 else PIECES[1])

    def a_arrive(q, zz):
        if CHUNKS[q][0] or zz:
            blk = a_block(q, y, zz)
            remote(blk, blk, a_s.at[q, zz], a_r.at[q, zz], dev(x, c, y, mir)).wait_recv()

    def gather_copy(q, up, ys, zz, frm, k, pieces):
        s, off, n = CHUNKS[q]
        blk = abuf.at[(x + s) % 4, ys * 2 + zz]
        to = (y + 1) % 4 if up else (y + 3) % 4
        start((blk, blk, off, n, g_s.at[q, k], g_r.at[q, frm, zz], dev(x, c, to, z)), pieces)

    def gather_start(q):
        for k, (up, zz) in enumerate(((True, 0), (False, 0), (False, 1), (True, 1))):
            if k == 0 or k == 2:
                a_arrive(q, zz)
            gather_copy(q, up, y, zz, 0 if up else 1, k, PIECES[2])

    def gather_wait(q, frm, zz):
        blk = a_block(q, (y + (3, 1, 2)[frm]) % 4, zz)
        remote(blk, blk, g_s.at[q, 0], g_r.at[q, frm, zz], dev(x, c, y, mir)).wait_recv()

    def gather_forward(q):
        gather_wait(q, 0, 0)
        gather_copy(q, True, (y + 3) % 4, 0, 2, 4, PIECES[3])
        gather_wait(q, 1, 1)
        gather_copy(q, False, (y + 1) % 4, 1, 2, 5, PIECES[3])

    def gather_rest(q):
        gather_wait(q, 0, 1)
        gather_wait(q, 1, 0)
        gather_wait(q, 2, 0)
        gather_wait(q, 2, 1)

    def product(q, j, dst, more=None):
        s, off, n = CHUNKS[q]
        left = jnp.concatenate([abuf[(x + s) % 4, k, pl.ds(off, n), :] for k in range(8)], axis=1)
        total = jnp.dot(left, bbuf[j], preferred_element_type=jnp.float32)
        for i in range(2):
            lines = pl.ds(BASE[q] + i, n, stride=2)
            part = total[:, i * 128:(i + 1) * 128]
            dst[lines, :] = part if more is None else part + more[lines, :]

    def lines_of(q):
        return pl.ds(BASE[q], 2 * CHUNKS[q][2])

    def partial_copy(q, j):
        return remote(cp.at[j, lines_of(q)], cr.at[j, lines_of(q)], p_s.at[q, j], p_r.at[q, j], dev(x, c, y, buddy))

    def partial_send(q, first=0, count=2):
        @pl.loop(first, first + count)
        def _(i):
            j = 1 - i
            product(q, j, cp.at[j])
            partial_copy(q, j).start()

    def final_copy(q, j):
        s, off, n = CHUNKS[q]
        src = cf.at[j, lines_of(q)]
        dst = out.at[x * 2 + par, pl.ds(2 * off, 2 * n)]
        if s == 0 and j == 0:
            return pltpu.make_async_copy(src, dst, o_s.at[q, j])
        return remote(src, dst, o_s.at[q, j], o_r.at[q, j], dev((x + s) % 4, c, y, mir if j else z))

    def final_arrive(q, j):
        s, off, n = CHUNKS[q]
        h = (x + 4 - s) % 4 * 2 + (1 - par if j else par)
        dst = out.at[h, pl.ds(2 * off, 2 * n)]
        remote(cf.at[j, lines_of(q)], dst, o_s.at[q, j], o_r.at[q, j], dev(x, c, y, mir)).wait_recv()

    def own(q, j):
        product(q, j + 2, cf.at[j])

    def finish(q, j):
        partial_copy(q, j).wait_recv()
        cf[j, lines_of(q), :] += cr[j, lines_of(q), :]
        final_copy(q, j).start()

    steps = dict(AS=a_start, BL=b_lay, BA=b_arrive, GS=gather_start, GF=gather_forward, GR=gather_rest)
    for step in PLAN:
        args = [int(d) for d in step if d.isdigit()]
        name = step.rstrip("0123456789")
        if name == "P":
            partial_send(args[0], *((1 - args[1], 1) if len(args) > 1 else ()))
        elif name == "BS":
            b_start(args[0], ((1, 3), (2, 0))[args[1]] if len(args) > 1 else (1, 3, 2, 0))
        elif name == "F":
            for j in args[1:] or (1, 0):
                partial_copy(args[0], j).wait_recv()
                product(args[0], j + 2, cf.at[j], cr.at[j])
                final_copy(args[0], j).start()
        elif name == "Z":
            for cp_ in sends:
                cp_.wait_send()
            b_wait_sends()
            b_forward_wait()
        elif name == "O":
            own(*args)
        elif name == "W":
            finish(*args)
        else:
            steps[name](*args)

    for q in range(NQ):
        for j in range(2):
            partial_copy(q, j).wait_send()
            if CHUNKS[q][0] == 0 and j == 0:
                final_copy(q, j).wait()
            else:
                final_copy(q, j).wait_send()
                final_arrive(q, j)

def per_device(amp, integrals, residual_in):
    irreps, blocks, blk, kb, _ = integrals.shape
    rows = blocks * blk
    left = integrals.reshape(irreps, rows * kb, blk)
    right = amp.reshape(kb * blk, 32, blk)
    res = residual_in.reshape(irreps, rows * 2, blk)
    dma = pltpu.SemaphoreType.DMA
    out = pl.pallas_call(
        kernel,
        out_shape=jax.ShapeDtypeStruct(res.shape, jnp.float32),
        in_specs=[pl.BlockSpec(memory_space=pl.ANY)] * 2,
        out_specs=pl.BlockSpec(memory_space=pl.ANY),
        scratch_shapes=[
            pltpu.VMEM(left.shape, jnp.bfloat16),
            pltpu.VMEM(right.shape, jnp.bfloat16),
            pltpu.VMEM((384, blk), jnp.float32),
            pltpu.VMEM((8192, blk), jnp.float32),
            pltpu.VMEM((8, rows, 256), jnp.bfloat16),
            pltpu.VMEM((4, 4, 256, 256), jnp.bfloat16),
            pltpu.VMEM((4, 8, rows, 256), jnp.bfloat16),
            pltpu.VMEM((4, 2048, 256), jnp.bfloat16),
            pltpu.VMEM((2, LINES, blk), jnp.float32),
            pltpu.VMEM((2, LINES, blk), jnp.float32),
            pltpu.VMEM((2, LINES, blk), jnp.float32),
            dma((2,)),
            dma((NQ, 2)), dma((NQ, 2)),
            dma((NQ, 6)), dma((NQ, 3, 2)),
            dma((4, 4)), dma((4, 2, 4)), dma((4, 4)),
            dma((NQ, 2)), dma((NQ, 2)),
            dma((NQ, 2)), dma((NQ, 2)),
        ],
        compiler_params=pltpu.CompilerParams(collective_id=0, has_side_effects=True, vmem_limit_bytes=36 << 20),
    )(pltpu.with_memory_space_constraint(left, pltpu.HBM), pltpu.with_memory_space_constraint(right, pltpu.HBM))
    return (res + out).reshape(residual_in.shape)


def solution(mesh):
    placed = (
        P("row", "col", None, None, None),
        P(None, "row", None, "col", None),
        P(None, "row", None, "col", None),
    )
    return jax.shard_map(
        per_device,
        mesh=mesh,
        in_specs=placed,
        out_specs=P(None, "row", None, "col", None),
        check_vma=False,
    )
```

```python
import jax
import jax.numpy as jnp
from jax import lax
from jax.experimental import pallas as pl
from jax.experimental.pallas import tpu as pltpu
from jax.sharding import PartitionSpec as P

MESH = pl.DeviceIdType.MESH
JXOR = (1, 2, 0, 3)
CHUNKS = (
    (0, 0, 192), (1, 0, 192), (1, 192, 192), (2, 0, 192), (2, 192, 192),
    (3, 0, 192), (3, 192, 192), (0, 192, 192),
)
NQ = len(CHUNKS)
BASE = tuple(2 * sum(n for _, _, n in CHUNKS[:q]) for q in range(NQ))
LINES = 2 * sum(n for _, _, n in CHUNKS)
PIECES = (4, 1, 1, 2)
PLAN = (
    "AS0", "BS1", "BL0", "BS0", "AS1", "AL2", "AL3", "AL4", "AL5", "AL6", "AL7", "BL3", "BL2", "GS0", "AS2",
    "BA1", "GF0", "AS3", "GS1", "GR0", "P01", "BA0", "AS4", "GS2", "GF1", "P00", "AS5", "GS3", "BS3", "BS2",
    "GF2", "GR1", "P1", "AS6", "GS4", "GF3", "GR2", "P2", "BA3", "BA2", "F01", "F00", "AS7", "GS5", "GF4", "GR3",
    "P3", "F11", "F10", "GS6", "GF5", "GR4", "P4", "F21", "F20", "GS7", "GF6", "GR5", "P5", "F31", "F30", "GF7",
    "GR6", "P6", "F41", "F40", "GR7", "P7", "F51", "F50", "O61", "O60", "O71", "O70", "Z", "W61", "W60", "W71",
    "W70",
)


def kernel(a_in, b_in, out, araw, braw, atmp, btmp, ast, bst, abuf, bbuf, cp, cr, cf,
           in_s, a_s, a_r, g_s, g_r, b_s, b_r, f_s, p_s, p_r, o_s, o_r):
    row, col = lax.axis_index("row"), lax.axis_index("col")
    x, c, y, z = row // 2, row % 2, col // 4, col % 4
    par = z // 2
    mir = 3 - z
    buddy = z + 1 - 2 * (z % 2)

    def dev(xx, cc, yy, zz):
        return (xx * 2 + cc, yy * 4 + zz)

    def xor(zz, j):
        lo, hi = zz % 2, zz // 2
        m = JXOR[j]
        lo = 1 - lo if m % 2 else lo
        hi = 1 - hi if m // 2 else hi
        return hi * 2 + lo

    def remote(src, dst, ss, rs, d):
        return pltpu.make_async_remote_copy(src, dst, ss, rs, device_id=d, device_id_type=MESH)

    b_load = pltpu.make_async_copy(b_in, braw, in_s.at[0])
    a_load = pltpu.make_async_copy(a_in, araw, in_s.at[1])
    b_load.start()
    a_load.start()
    barrier = pltpu.get_barrier_semaphore()
    peers = []
    for d in range(4):
        for zz in (z, mir):
            if d or zz is mir:
                peers.append(dev((x + d) % 4, c, y, zz))
            if d:
                peers.append(dev(x, c, (y + d) % 4, zz))
    peers.append(dev(x, 1 - c, y, z))
    peers.append(dev(x, c, y, buddy))
    for d in peers:
        pl.semaphore_signal(barrier, inc=1, device_id=d, device_id_type=MESH)
    b_load.wait()

    @pl.loop(0, 8)
    def _(t):
        ks = pl.ds(t * 32, 32)
        btmp[pl.ds(t * 1024, 1024), :] = braw[ks].astype(jnp.float32).reshape(1024, 128)

    def b_lay(j):
        zj = jnp.where(c == par, xor(z, j), xor(mir, j))
        for yd in range(4):
            for i in range(2):
                lines = btmp[pl.ds(yd * 8 + zj * 2 + i, 256, stride=32), :]
                bst[j, yd, :, i * 128:(i + 1) * 128] = lines.astype(jnp.bfloat16)

    def a_lay(q):
        dx, off, n = CHUNKS[q]
        hx = (x + 4 - dx) % 4
        for zz in range(2):
            h = hx * 2 + (1 - par if zz else par)
            atmp[pl.ds(0, 2 * n), :] = araw[h, pl.ds(2 * off, 2 * n), :].astype(jnp.float32)
            for i in range(2):
                lines = atmp[pl.ds(i, n, stride=2), :].astype(jnp.bfloat16)
                lanes = slice(i * 128, (i + 1) * 128)
                if dx == 0 and zz == 0:
                    abuf[x, y * 2, off:off + n, lanes] = lines
                else:
                    ast[h, off:off + n, lanes] = lines

    b_lay(1)
    a_load.wait()
    a_lay(0)
    pl.semaphore_wait(barrier, len(peers))

    sends = []

    def start(blocks, pieces):
        src, dst, off, n, ss, rs, d = blocks
        for k in range(pieces):
            rows = pl.ds(off + k * (n // pieces), n // pieces)
            remote(src.at[rows], dst.at[rows], ss, rs, d).start()
        rows = pl.ds(off, n)
        sends.append(remote(src.at[rows], dst.at[rows], ss, rs, d))

    def b_block(j, ys, zz):
        return bbuf.at[j, pl.ds(pl.multiple_of((ys * 2 + zz) * 256, 256), 256)]

    def b_start(j, dys=(1, 3, 2, 0)):
        for dy in dys:
            yd = (y + dy) % 4

            def go(zd, zz, local):
                src = bst.at[j, yd]
                dst = b_block(j, y, zz)
                if local:
                    pltpu.make_async_copy(src, dst, b_r.at[y, zz, j]).start()
                else:
                    remote(src, dst, b_s.at[dy, j], b_r.at[y, zz, j], dev(x, c, yd, zd)).start()

            @pl.when(c == par)
            def _():
                go(z, 0, dy == 0)

            @pl.when(c != par)
            def _():
                go(mir, 1, False)

    def b_wait_sends():
        for j in range(4):
            for dy in range(4):
                cp_ = remote(bst.at[0, 0], b_block(0, 0, 0), b_s.at[dy, j], b_r.at[0, 0, j], dev(x, c, y, mir))
                if dy == 0:
                    @pl.when(c != par)
                    def _():
                        cp_.wait_send()
                else:
                    cp_.wait_send()

    def b_pair(j, dy):
        ys = (y + dy) % 4
        blk = bbuf.at[j, pl.ds(pl.multiple_of(ys * 512, 512), 512)]
        return remote(blk, blk, f_s.at[dy, j], b_r.at[ys, 0, j], dev(x, 1 - c, y, z))

    def b_arrive(j):
        for dy in (0, 1, 3, 2):
            ys = (y + dy) % 4

            @pl.when(c == par)
            def _():
                for zz in range(2):
                    blk = b_block(j, ys, zz)
                    remote(blk, blk, f_s.at[dy, j], b_r.at[ys, zz, j], dev(x, 1 - c, y, z)).wait_recv()
                b_pair(j, dy).start()

            @pl.when(c != par)
            def _():
                b_pair(j, dy).wait_recv()

    def b_forward_wait():
        @pl.when(c == par)
        def _():
            for j in range(4):
                for dy in range(4):
                    b_pair(j, dy).wait_send()

    def a_block(q, ys, zz):
        s, off, n = CHUNKS[q]
        return abuf.at[(x + s) % 4, ys * 2 + zz, pl.ds(off, n)]

    def a_start(q):
        dx, off, n = CHUNKS[q]
        hx = (x + 4 - dx) % 4
        if q and "AL" + str(q) not in PLAN:
            a_lay(q)
        for zz in (1, 0):
            if dx or zz:
                zd = mir if zz else z
                start((ast.at[hx * 2 + zd // 2], abuf.at[x, y * 2 + zz], off, n,
                       a_s.at[q, zz], a_r.at[q, zz], dev(hx, c, y, zd)), PIECES[0] if q == 0 else PIECES[1])

    def a_arrive(q, zz):
        if CHUNKS[q][0] or zz:
            blk = a_block(q, y, zz)
            remote(blk, blk, a_s.at[q, zz], a_r.at[q, zz], dev(x, c, y, mir)).wait_recv()

    def gather_copy(q, up, ys, zz, frm, k, pieces):
        s, off, n = CHUNKS[q]
        blk = abuf.at[(x + s) % 4, ys * 2 + zz]
        to = (y + 1) % 4 if up else (y + 3) % 4
        start((blk, blk, off, n, g_s.at[q, k], g_r.at[q, frm, zz], dev(x, c, to, z)), pieces)

    def gather_start(q):
        for k, (up, zz) in enumerate(((True, 0), (False, 0), (False, 1), (True, 1))):
            if k == 0 or k == 2:
                a_arrive(q, zz)
            gather_copy(q, up, y, zz, 0 if up else 1, k, PIECES[2])

    def gather_wait(q, frm, zz):
        blk = a_block(q, (y + (3, 1, 2)[frm]) % 4, zz)
        remote(blk, blk, g_s.at[q, 0], g_r.at[q, frm, zz], dev(x, c, y, mir)).wait_recv()

    def gather_forward(q):
        gather_wait(q, 0, 0)
        gather_copy(q, True, (y + 3) % 4, 0, 2, 4, PIECES[3])
        gather_wait(q, 1, 1)
        gather_copy(q, False, (y + 1) % 4, 1, 2, 5, PIECES[3])

    def gather_rest(q):
        gather_wait(q, 0, 1)
        gather_wait(q, 1, 0)
        gather_wait(q, 2, 0)
        gather_wait(q, 2, 1)

    def product(q, j, dst, more=None):
        s, off, n = CHUNKS[q]
        left = jnp.concatenate([abuf[(x + s) % 4, k, pl.ds(off, n), :] for k in range(8)], axis=1)
        total = jnp.dot(left, bbuf[j], preferred_element_type=jnp.float32)
        for i in range(2):
            lines = pl.ds(BASE[q] + i, n, stride=2)
            part = total[:, i * 128:(i + 1) * 128]
            dst[lines, :] = part if more is None else part + more[lines, :]

    def lines_of(q):
        return pl.ds(BASE[q], 2 * CHUNKS[q][2])

    def partial_copy(q, j):
        return remote(cp.at[j, lines_of(q)], cr.at[j, lines_of(q)], p_s.at[q, j], p_r.at[q, j], dev(x, c, y, buddy))

    def partial_send(q, first=0, count=2):
        @pl.loop(first, first + count)
        def _(i):
            j = 1 - i
            product(q, j, cp.at[j])
            partial_copy(q, j).start()

    def final_copy(q, j):
        s, off, n = CHUNKS[q]
        src = cf.at[j, lines_of(q)]
        dst = out.at[x * 2 + par, pl.ds(2 * off, 2 * n)]
        if s == 0 and j == 0:
            return pltpu.make_async_copy(src, dst, o_s.at[q, j])
        return remote(src, dst, o_s.at[q, j], o_r.at[q, j], dev((x + s) % 4, c, y, mir if j else z))

    def final_arrive(q, j):
        s, off, n = CHUNKS[q]
        h = (x + 4 - s) % 4 * 2 + (1 - par if j else par)
        dst = out.at[h, pl.ds(2 * off, 2 * n)]
        remote(cf.at[j, lines_of(q)], dst, o_s.at[q, j], o_r.at[q, j], dev(x, c, y, mir)).wait_recv()

    def own(q, j):
        product(q, j + 2, cf.at[j])

    def finish(q, j):
        partial_copy(q, j).wait_recv()
        cf[j, lines_of(q), :] += cr[j, lines_of(q), :]
        final_copy(q, j).start()

    steps = dict(AL=a_lay, AS=a_start, BL=b_lay, BA=b_arrive, GS=gather_start, GF=gather_forward, GR=gather_rest)
    for step in PLAN:
        args = [int(d) for d in step if d.isdigit()]
        name = step.rstrip("0123456789")
        if name == "P":
            partial_send(args[0], *((1 - args[1], 1) if len(args) > 1 else ()))
        elif name == "BS":
            b_start(args[0], ((1, 3), (2, 0))[args[1]] if len(args) > 1 else (1, 3, 2, 0))
        elif name == "F":
            for j in args[1:] or (1, 0):
                partial_copy(args[0], j).wait_recv()
                product(args[0], j + 2, cf.at[j], cr.at[j])
                final_copy(args[0], j).start()
        elif name == "Z":
            for cp_ in sends:
                cp_.wait_send()
            b_wait_sends()
            b_forward_wait()
        elif name == "O":
            own(*args)
        elif name == "W":
            finish(*args)
        else:
            steps[name](*args)

    for q in range(NQ):
        for j in range(2):
            partial_copy(q, j).wait_send()
            if CHUNKS[q][0] == 0 and j == 0:
                final_copy(q, j).wait()
            else:
                final_copy(q, j).wait_send()
                final_arrive(q, j)

def per_device(amp, integrals, residual_in):
    irreps, blocks, blk, kb, _ = integrals.shape
    rows = blocks * blk
    left = integrals.reshape(irreps, rows * kb, blk)
    right = amp.reshape(kb * blk, 32, blk)
    res = residual_in.reshape(irreps, rows * 2, blk)
    dma = pltpu.SemaphoreType.DMA
    out = pl.pallas_call(
        kernel,
        out_shape=jax.ShapeDtypeStruct(res.shape, jnp.float32),
        in_specs=[pl.BlockSpec(memory_space=pl.ANY)] * 2,
        out_specs=pl.BlockSpec(memory_space=pl.ANY),
        scratch_shapes=[
            pltpu.VMEM(left.shape, jnp.bfloat16),
            pltpu.VMEM(right.shape, jnp.bfloat16),
            pltpu.VMEM((384, blk), jnp.float32),
            pltpu.VMEM((8192, blk), jnp.float32),
            pltpu.VMEM((8, rows, 256), jnp.bfloat16),
            pltpu.VMEM((4, 4, 256, 256), jnp.bfloat16),
            pltpu.VMEM((4, 8, rows, 256), jnp.bfloat16),
            pltpu.VMEM((4, 2048, 256), jnp.bfloat16),
            pltpu.VMEM((2, LINES, blk), jnp.float32),
            pltpu.VMEM((2, LINES, blk), jnp.float32),
            pltpu.VMEM((2, LINES, blk), jnp.float32),
            dma((2,)),
            dma((NQ, 2)), dma((NQ, 2)),
            dma((NQ, 6)), dma((NQ, 3, 2)),
            dma((4, 4)), dma((4, 2, 4)), dma((4, 4)),
            dma((NQ, 2)), dma((NQ, 2)),
            dma((NQ, 2)), dma((NQ, 2)),
        ],
        compiler_params=pltpu.CompilerParams(collective_id=0, has_side_effects=True, vmem_limit_bytes=36 << 20),
    )(pltpu.with_memory_space_constraint(left, pltpu.HBM), pltpu.with_memory_space_constraint(right, pltpu.HBM))
    return (res + out).reshape(residual_in.shape)


def solution(mesh):
    placed = (
        P("row", "col", None, None, None),
        P(None, "row", None, "col", None),
        P(None, "row", None, "col", None),
    )
    return jax.shard_map(
        per_device,
        mesh=mesh,
        in_specs=placed,
        out_specs=P(None, "row", None, "col", None),
        check_vma=False,
    )
```

```python
import jax
import jax.numpy as jnp
from jax import lax
from jax.experimental import pallas as pl
from jax.experimental.pallas import tpu as pltpu
from jax.sharding import PartitionSpec as P

MESH = pl.DeviceIdType.MESH
JXOR = (1, 2, 0, 3)
CHUNKS = (
    (0, 0, 192), (1, 0, 192), (1, 192, 192), (2, 0, 192), (2, 192, 192),
    (3, 0, 192), (3, 192, 192), (0, 192, 192),
)
NQ = len(CHUNKS)
BASE = tuple(2 * sum(n for _, _, n in CHUNKS[:q]) for q in range(NQ))
LINES = 2 * sum(n for _, _, n in CHUNKS)
PIECES = (4, 1, 1, 2)
PLAN = (
    "AS0", "BS1", "BL0", "BS0", "AS1", "AL2", "AL3", "AL4", "AL5", "AL6", "AL7", "BL3", "BL2", "GS0", "AS2",
    "BA1", "GF0", "AS3", "GS1", "GR0", "P01", "BA0", "AS4", "GS2", "GF1", "P00", "AS5", "GS3", "GF2", "BS3",
    "BS2", "GR1", "P1", "AS6", "GS4", "GF3", "GR2", "P2", "BA3", "BA2", "F01", "F00", "AS7", "GS5", "GF4", "GR3",
    "P3", "F11", "F10", "GS6", "GF5", "GR4", "P4", "F21", "F20", "GS7", "GF6", "GR5", "P5", "F31", "F30", "GF7",
    "GR6", "P6", "F41", "F40", "GR7", "P7", "F51", "F50", "O61", "O60", "O71", "O70", "Z", "W61", "W60", "W71",
    "W70",
)


def kernel(a_in, b_in, out, araw, braw, atmp, btmp, ast, bst, abuf, bbuf, cp, cr, cf,
           in_s, a_s, a_r, g_s, g_r, b_s, b_r, f_s, p_s, p_r, o_s, o_r):
    row, col = lax.axis_index("row"), lax.axis_index("col")
    x, c, y, z = row // 2, row % 2, col // 4, col % 4
    par = z // 2
    mir = 3 - z
    buddy = z + 1 - 2 * (z % 2)

    def dev(xx, cc, yy, zz):
        return (xx * 2 + cc, yy * 4 + zz)

    def xor(zz, j):
        lo, hi = zz % 2, zz // 2
        m = JXOR[j]
        lo = 1 - lo if m % 2 else lo
        hi = 1 - hi if m // 2 else hi
        return hi * 2 + lo

    def remote(src, dst, ss, rs, d):
        return pltpu.make_async_remote_copy(src, dst, ss, rs, device_id=d, device_id_type=MESH)

    b_load = pltpu.make_async_copy(b_in, braw, in_s.at[0])
    a_load = pltpu.make_async_copy(a_in, araw, in_s.at[1])
    b_load.start()
    a_load.start()
    barrier = pltpu.get_barrier_semaphore()
    peers = []
    for d in range(4):
        for zz in (z, mir):
            if d or zz is mir:
                peers.append(dev((x + d) % 4, c, y, zz))
            if d:
                peers.append(dev(x, c, (y + d) % 4, zz))
    peers.append(dev(x, 1 - c, y, z))
    peers.append(dev(x, c, y, buddy))
    for d in peers:
        pl.semaphore_signal(barrier, inc=1, device_id=d, device_id_type=MESH)
    b_load.wait()

    @pl.loop(0, 8)
    def _(t):
        ks = pl.ds(t * 32, 32)
        btmp[pl.ds(t * 1024, 1024), :] = braw[ks].astype(jnp.float32).reshape(1024, 128)

    def b_lay(j):
        zj = jnp.where(c == par, xor(z, j), xor(mir, j))
        for yd in range(4):
            for i in range(2):
                lines = btmp[pl.ds(yd * 8 + zj * 2 + i, 256, stride=32), :]
                bst[j, yd, :, i * 128:(i + 1) * 128] = lines.astype(jnp.bfloat16)

    def a_lay(q):
        dx, off, n = CHUNKS[q]
        hx = (x + 4 - dx) % 4
        for zz in range(2):
            h = hx * 2 + (1 - par if zz else par)
            atmp[pl.ds(0, 2 * n), :] = araw[h, pl.ds(2 * off, 2 * n), :].astype(jnp.float32)
            for i in range(2):
                lines = atmp[pl.ds(i, n, stride=2), :].astype(jnp.bfloat16)
                lanes = slice(i * 128, (i + 1) * 128)
                if dx == 0 and zz == 0:
                    abuf[x, y * 2, off:off + n, lanes] = lines
                else:
                    ast[h, off:off + n, lanes] = lines

    b_lay(1)
    a_load.wait()
    a_lay(0)
    pl.semaphore_wait(barrier, len(peers))

    sends = []

    def start(blocks, pieces):
        src, dst, off, n, ss, rs, d = blocks
        for k in range(pieces):
            rows = pl.ds(off + k * (n // pieces), n // pieces)
            remote(src.at[rows], dst.at[rows], ss, rs, d).start()
        rows = pl.ds(off, n)
        sends.append(remote(src.at[rows], dst.at[rows], ss, rs, d))

    def b_block(j, ys, zz):
        return bbuf.at[j, pl.ds(pl.multiple_of((ys * 2 + zz) * 256, 256), 256)]

    def b_start(j, dys=(1, 3, 2, 0)):
        for dy in dys:
            yd = (y + dy) % 4

            def go(zd, zz, local):
                src = bst.at[j, yd]
                dst = b_block(j, y, zz)
                if local:
                    pltpu.make_async_copy(src, dst, b_r.at[y, zz, j]).start()
                else:
                    remote(src, dst, b_s.at[dy, j], b_r.at[y, zz, j], dev(x, c, yd, zd)).start()

            @pl.when(c == par)
            def _():
                go(z, 0, dy == 0)

            @pl.when(c != par)
            def _():
                go(mir, 1, False)

    def b_wait_sends():
        for j in range(4):
            for dy in range(4):
                cp_ = remote(bst.at[0, 0], b_block(0, 0, 0), b_s.at[dy, j], b_r.at[0, 0, j], dev(x, c, y, mir))
                if dy == 0:
                    @pl.when(c != par)
                    def _():
                        cp_.wait_send()
                else:
                    cp_.wait_send()

    def b_pair(j, dy):
        ys = (y + dy) % 4
        blk = bbuf.at[j, pl.ds(pl.multiple_of(ys * 512, 512), 512)]
        return remote(blk, blk, f_s.at[dy, j], b_r.at[ys, 0, j], dev(x, 1 - c, y, z))

    def b_arrive(j):
        for dy in (0, 1, 3, 2):
            ys = (y + dy) % 4

            @pl.when(c == par)
            def _():
                for zz in range(2):
                    blk = b_block(j, ys, zz)
                    remote(blk, blk, f_s.at[dy, j], b_r.at[ys, zz, j], dev(x, 1 - c, y, z)).wait_recv()
                b_pair(j, dy).start()

            @pl.when(c != par)
            def _():
                b_pair(j, dy).wait_recv()

    def b_forward_wait():
        @pl.when(c == par)
        def _():
            for j in range(4):
                for dy in range(4):
                    b_pair(j, dy).wait_send()

    def a_block(q, ys, zz):
        s, off, n = CHUNKS[q]
        return abuf.at[(x + s) % 4, ys * 2 + zz, pl.ds(off, n)]

    def a_start(q):
        dx, off, n = CHUNKS[q]
        hx = (x + 4 - dx) % 4
        if q and "AL" + str(q) not in PLAN:
            a_lay(q)
        for zz in (1, 0):
            if dx or zz:
                zd = mir if zz else z
                start((ast.at[hx * 2 + zd // 2], abuf.at[x, y * 2 + zz], off, n,
                       a_s.at[q, zz], a_r.at[q, zz], dev(hx, c, y, zd)), PIECES[0] if q == 0 else PIECES[1])

    def a_arrive(q, zz):
        if CHUNKS[q][0] or zz:
            blk = a_block(q, y, zz)
            remote(blk, blk, a_s.at[q, zz], a_r.at[q, zz], dev(x, c, y, mir)).wait_recv()

    def gather_copy(q, up, ys, zz, frm, k, pieces):
        s, off, n = CHUNKS[q]
        blk = abuf.at[(x + s) % 4, ys * 2 + zz]
        to = (y + 1) % 4 if up else (y + 3) % 4
        start((blk, blk, off, n, g_s.at[q, k], g_r.at[q, frm, zz], dev(x, c, to, z)), pieces)

    def gather_start(q):
        for k, (up, zz) in enumerate(((True, 0), (False, 0), (False, 1), (True, 1))):
            if k == 0 or k == 2:
                a_arrive(q, zz)
            gather_copy(q, up, y, zz, 0 if up else 1, k, PIECES[2])

    def gather_wait(q, frm, zz):
        blk = a_block(q, (y + (3, 1, 2)[frm]) % 4, zz)
        remote(blk, blk, g_s.at[q, 0], g_r.at[q, frm, zz], dev(x, c, y, mir)).wait_recv()

    def gather_forward(q):
        gather_wait(q, 0, 0)
        gather_copy(q, True, (y + 3) % 4, 0, 2, 4, PIECES[3])
        gather_wait(q, 1, 1)
        gather_copy(q, False, (y + 1) % 4, 1, 2, 5, PIECES[3])

    def gather_rest(q):
        gather_wait(q, 0, 1)
        gather_wait(q, 1, 0)
        gather_wait(q, 2, 0)
        gather_wait(q, 2, 1)

    def product(q, j, dst, more=None):
        s, off, n = CHUNKS[q]
        left = jnp.concatenate([abuf[(x + s) % 4, k, pl.ds(off, n), :] for k in range(8)], axis=1)
        total = jnp.dot(left, bbuf[j], preferred_element_type=jnp.float32)
        for i in range(2):
            lines = pl.ds(BASE[q] + i, n, stride=2)
            part = total[:, i * 128:(i + 1) * 128]
            dst[lines, :] = part if more is None else part + more[lines, :]

    def lines_of(q):
        return pl.ds(BASE[q], 2 * CHUNKS[q][2])

    def partial_copy(q, j):
        return remote(cp.at[j, lines_of(q)], cr.at[j, lines_of(q)], p_s.at[q, j], p_r.at[q, j], dev(x, c, y, buddy))

    def partial_send(q, first=0, count=2):
        @pl.loop(first, first + count)
        def _(i):
            j = 1 - i
            product(q, j, cp.at[j])
            partial_copy(q, j).start()

    def final_copy(q, j):
        s, off, n = CHUNKS[q]
        src = cf.at[j, lines_of(q)]
        dst = out.at[x * 2 + par, pl.ds(2 * off, 2 * n)]
        if s == 0 and j == 0:
            return pltpu.make_async_copy(src, dst, o_s.at[q, j])
        return remote(src, dst, o_s.at[q, j], o_r.at[q, j], dev((x + s) % 4, c, y, mir if j else z))

    def final_arrive(q, j):
        s, off, n = CHUNKS[q]
        h = (x + 4 - s) % 4 * 2 + (1 - par if j else par)
        dst = out.at[h, pl.ds(2 * off, 2 * n)]
        remote(cf.at[j, lines_of(q)], dst, o_s.at[q, j], o_r.at[q, j], dev(x, c, y, mir)).wait_recv()

    def own(q, j):
        product(q, j + 2, cf.at[j])

    def finish(q, j):
        partial_copy(q, j).wait_recv()
        cf[j, lines_of(q), :] += cr[j, lines_of(q), :]
        final_copy(q, j).start()

    steps = dict(AL=a_lay, AS=a_start, BL=b_lay, BA=b_arrive, GS=gather_start, GF=gather_forward, GR=gather_rest)
    for step in PLAN:
        args = [int(d) for d in step if d.isdigit()]
        name = step.rstrip("0123456789")
        if name == "P":
            partial_send(args[0], *((1 - args[1], 1) if len(args) > 1 else ()))
        elif name == "BS":
            b_start(args[0], ((1, 3), (2, 0))[args[1]] if len(args) > 1 else (1, 3, 2, 0))
        elif name == "F":
            for j in args[1:] or (1, 0):
                partial_copy(args[0], j).wait_recv()
                product(args[0], j + 2, cf.at[j], cr.at[j])
                final_copy(args[0], j).start()
        elif name == "Z":
            for cp_ in sends:
                cp_.wait_send()
            b_wait_sends()
            b_forward_wait()
        elif name == "O":
            own(*args)
        elif name == "W":
            finish(*args)
        else:
            steps[name](*args)

    for q in range(NQ):
        for j in range(2):
            partial_copy(q, j).wait_send()
            if CHUNKS[q][0] == 0 and j == 0:
                final_copy(q, j).wait()
            else:
                final_copy(q, j).wait_send()
                final_arrive(q, j)

def per_device(amp, integrals, residual_in):
    irreps, blocks, blk, kb, _ = integrals.shape
    rows = blocks * blk
    left = integrals.reshape(irreps, rows * kb, blk)
    right = amp.reshape(kb * blk, 32, blk)
    res = residual_in.reshape(irreps, rows * 2, blk)
    dma = pltpu.SemaphoreType.DMA
    out = pl.pallas_call(
        kernel,
        out_shape=jax.ShapeDtypeStruct(res.shape, jnp.float32),
        in_specs=[pl.BlockSpec(memory_space=pl.ANY)] * 2,
        out_specs=pl.BlockSpec(memory_space=pl.ANY),
        scratch_shapes=[
            pltpu.VMEM(left.shape, jnp.bfloat16),
            pltpu.VMEM(right.shape, jnp.bfloat16),
            pltpu.VMEM((384, blk), jnp.float32),
            pltpu.VMEM((8192, blk), jnp.float32),
            pltpu.VMEM((8, rows, 256), jnp.bfloat16),
            pltpu.VMEM((4, 4, 256, 256), jnp.bfloat16),
            pltpu.VMEM((4, 8, rows, 256), jnp.bfloat16),
            pltpu.VMEM((4, 2048, 256), jnp.bfloat16),
            pltpu.VMEM((2, LINES, blk), jnp.float32),
            pltpu.VMEM((2, LINES, blk), jnp.float32),
            pltpu.VMEM((2, LINES, blk), jnp.float32),
            dma((2,)),
            dma((NQ, 2)), dma((NQ, 2)),
            dma((NQ, 6)), dma((NQ, 3, 2)),
            dma((4, 4)), dma((4, 2, 4)), dma((4, 4)),
            dma((NQ, 2)), dma((NQ, 2)),
            dma((NQ, 2)), dma((NQ, 2)),
        ],
        compiler_params=pltpu.CompilerParams(collective_id=0, has_side_effects=True, vmem_limit_bytes=36 << 20),
    )(pltpu.with_memory_space_constraint(left, pltpu.HBM), pltpu.with_memory_space_constraint(right, pltpu.HBM))
    return (res + out).reshape(residual_in.shape)


def solution(mesh):
    placed = (
        P("row", "col", None, None, None),
        P(None, "row", None, "col", None),
        P(None, "row", None, "col", None),
    )
    return jax.shard_map(
        per_device,
        mesh=mesh,
        in_specs=placed,
        out_specs=P(None, "row", None, "col", None),
        check_vma=False,
    )
```
